256 devices in a mesh: cells: 32 (over y, x, core), comp: 8 (over z).
Axes of the slice: x: 4, y: 4, z: 8, core: 2. Of those that a mesh axis runs over, the one named last changes fastest.
Arguments:
- factor_field: float32 [16, 1024, 256], P(None, ('cells', 'comp')), may hold values from -90 to 90
- profile: float32 [512, 128], P('comp'), may hold values from -4 to 4
- mixing: float32 [16, 512], P(None, 'comp'), may hold values from -1.5 to 1.5
- factor_mom: float32 [16, 1024, 256], P(None, ('cells', 'comp')), may hold values from -6 to 6
- profile_mom: float32 [512, 128], P('comp'), may hold values from -6 to 6
- mixing_mom: float32 [16, 512], P(None, 'comp'), may hold values from -6 to 6
- field_tau: float32 [16], replicated, may hold values from 0.5 to 5
- counts: int32 [128, 1024, 256], P(None, 'cells'), may hold values from 0 to 15
- land_mask: int32 [1024, 256], P('cells'), may hold values 0 or 1
- log_exposure: float32 [1024, 256], P('cells'), may hold values from -4 to -2
Outputs:
- new_field: float32 [16, 1024, 256], P(None, ('cells', 'comp'))
- new_profile: float32 [512, 128], P('comp')
- new_mixing: float32 [16, 512], P(None, 'comp')
- new_factor_mom: float32 [16, 1024, 256], P(None, ('cells', 'comp'))
- new_profile_mom: float32 [512, 128], P('comp')
- new_mixing_mom: float32 [16, 512], P(None, 'comp')
- hamiltonian: float32 [], replicated
The draws below stay inside these ranges and needn't reach their ends.
All inputs are finite; a program needn't handle non-finite values. No bound on the sum of `land_mask` on one device may be relied on, other than what follows from the above.
Results may differ from the reference program's by a relative error of at most 0.0003.
Values sent between devices are 32-bit elements; how exact they have to be, the bound alone decides.
A program may use at most 64 MiB of HBM per device.

```python
import math
import jax
import jax.numpy as jnp
from jax import lax

FAC = 16
K = 128
COMP = 512
RX = 32
GY = 256
GX = 1024
N_CELLS = 32


def draw_counts(key, part):
    level_key = jax.random.fold_in(key, 11)
    spot_key = jax.random.fold_in(key, 23)
    empty_key = jax.random.fold_in(key, 37)
    cells_all = GX * GY
    ticket = jax.random.randint(level_key, (K, cells_all), 0, 10000)
    sparse = (ticket >= 7400).astype(jnp.int32) + (ticket >= 9600).astype(jnp.int32)
    sparse = sparse + (ticket >= 9950).astype(jnp.int32) + (ticket >= 9995).astype(jnp.int32)
    hot_cell = jax.random.randint(spot_key, (K,), 0, cells_all)
    empty_cell = (hot_cell + 1 + jax.random.randint(empty_key, (K,), 0, cells_all - 1)) % cells_all
    category_ids = jnp.arange(K, dtype=jnp.int32)
    sparse = sparse.at[category_ids, empty_cell].set(0)
    sparse = sparse.at[category_ids, hot_cell].set(15)
    return sparse.reshape(K, GX, GY)


def draw_factor_field(key, part):
    base_key = jax.random.fold_in(key, 41)
    place_key = jax.random.fold_in(key, 43)
    power_key = jax.random.fold_in(key, 47)
    sign_key = jax.random.fold_in(key, 53)
    cells_all = GX * GY
    spikes = 8
    base = jnp.clip(jax.random.normal(base_key, (FAC, cells_all), jnp.float32), -6.0, 6.0)
    places = jax.random.permutation(place_key, cells_all)[:spikes].astype(jnp.int32)
    power = jax.random.uniform(power_key, (spikes,), jnp.float32, 40.0, 90.0)
    signs = jnp.where(jax.random.bernoulli(sign_key, 0.5, (FAC, spikes)), 1.0, -1.0).astype(jnp.float32)
    base = base.at[:, places].set(signs * power[None, :])
    return base.reshape(FAC, GX, GY).astype(jnp.float32)


def plant(values, stream_key, low, high):
    place = [jax.random.randint(jax.random.fold_in(stream_key, axis), (), 0, length) for axis, length in enumerate(values.shape)]
    main_axis = values.shape.index(max(values.shape))
    neighbour = place[:main_axis] + [(place[main_axis] + 1) % values.shape[main_axis]] + place[main_axis + 1:]
    return values.at[tuple(place)].set(low).at[tuple(neighbour)].set(high)


def shard_levels(rng, dims, shards, low, largest):
    loudness, own = 1.0, jax.random.fold_in(rng, 6)
    for dim, parts in shards:
        draws = jnp.exp(jax.random.uniform(jax.random.fold_in(own, dim), (parts,), jnp.float32, low / len(shards), largest / len(shards)))
        loudness = loudness * jnp.repeat(draws, dims[dim] // parts).reshape([-1 if axis == dim else 1 for axis in range(len(dims))])
    return loudness


def bell_draw(stream_key, shape, scale, bound, shards=(), kind=jnp.bfloat16):
    gain = shard_levels(stream_key, shape, shards, -0.22, 0.18) if shards else 1.0
    drawn = jax.random.normal(stream_key, shape, jnp.float32) * scale * gain
    return jnp.minimum(jnp.maximum(drawn, -bound), bound).astype(kind)


def setup_inputs(seed: int = 0) -> dict:
    seeds = jax.random.split(jax.random.key(seed), 11)
    return {
        "factor_field": draw_factor_field(jax.random.fold_in(seeds[10], 71), 0),
        "profile": bell_draw(seeds[1], (COMP, K), 1.0, 4.0, ((0, 8),), jnp.float32),
        "mixing": bell_draw(seeds[2], (FAC, COMP), FAC ** -0.5, 1.5, ((1, 8),), jnp.float32),
        "factor_mom": bell_draw(seeds[3], (FAC, GX, GY), 1.0, 6.0, ((1, 256),), jnp.float32),
        "profile_mom": bell_draw(seeds[4], (COMP, K), 1.0, 6.0, ((0, 8),), jnp.float32),
        "mixing_mom": bell_draw(seeds[5], (FAC, COMP), 1.0, 6.0, ((1, 8),), jnp.float32),
        "field_tau": jnp.clip(jnp.exp(jax.random.uniform(seeds[6], (FAC,), jnp.float32, math.log(0.5), math.log(5.0))), 0.5, 5.0),
        "counts": draw_counts(jax.random.fold_in(seeds[10], 71), 0),
        "land_mask": plant((jax.random.randint(seeds[8], (GX, GY), 0, 4) < 3).astype(jnp.int32), jax.random.fold_in(seeds[8], 1), 0, 1),
        "log_exposure": jnp.clip(-4.0 + 2.0 * jax.random.uniform(seeds[9], (GX, GY), jnp.float32) ** shard_levels(seeds[9], (GX, GY), ((0, 32),), -0.2, 0.2), -4.0, -2.0),
    }


def field_prior(padded, land_pad, field_tau):
    ridge = 0.1
    step_x = padded[:, 1:, :] - padded[:, :-1, :]
    edge_x = land_pad[1:, :] * land_pad[:-1, :]
    flux_x = edge_x[None, :, :] * step_x
    centre = padded[:, 1:-1, :]
    land_mid = land_pad[1:-1, :]
    step_y = centre[:, :, 1:] - centre[:, :, :-1]
    edge_y = land_mid[:, 1:] * land_mid[:, :-1]
    flux_y = edge_y[None, :, :] * step_y
    lap_x = flux_x[:, :-1, :] - flux_x[:, 1:, :]
    lap_y = jnp.pad(flux_y, ((0, 0), (0, 0), (1, 0))) - jnp.pad(flux_y, ((0, 0), (0, 0), (0, 1)))
    tau_cube = field_tau[:, None, None]
    grad = -tau_cube * (lap_x + lap_y + ridge * centre)
    energy = 0.5 * jnp.sum(tau_cube * (flux_x[:, 1:, :] * step_x[:, 1:, :]))
    energy = energy + 0.5 * jnp.sum(tau_cube * (flux_y * step_y))
    energy = energy + 0.5 * ridge * jnp.sum(tau_cube * (centre * centre))
    return grad, energy


def tile_scores(flat_tile, count_rows, exposure, profile, mixing):
    prof_exp = jnp.exp(profile)
    rate_total = jnp.sum(prof_exp, axis=1)
    mix_logit = jnp.dot(mixing.T, flat_tile, precision=lax.Precision.HIGHEST)
    fit_score = jnp.dot(profile, count_rows, precision=lax.Precision.HIGHEST) - rate_total[:, None] * exposure[None, :]
    return mix_logit, mix_logit + fit_score


def tile_grads(flat_tile, count_rows, land_weight, exposure, mixing, mix_logit, joint_score, log_mix, log_joint):
    prior_share = jnp.exp(mix_logit - log_mix[None, :])
    posterior = jnp.exp(joint_score - log_joint[None, :])
    post_land = posterior * land_weight[None, :]
    gap_weight = (posterior - prior_share) * land_weight[None, :]
    grad_counts = jnp.dot(post_land, count_rows.T, precision=lax.Precision.HIGHEST)
    rate_mass = jnp.sum(post_land * exposure[None, :], axis=1)
    grad_mix = jnp.dot(flat_tile, gap_weight.T, precision=lax.Precision.HIGHEST)
    field_lik = jnp.dot(mixing, gap_weight, precision=lax.Precision.HIGHEST)
    log_dens = jnp.sum(land_weight * (log_joint - log_mix))
    return grad_counts, rate_mass, grad_mix, field_lik, log_dens


def log_terms(factor_field, profile, mixing, counts, land_mask, log_exposure, field_tau):
    nfac = factor_field.shape[0]
    ncat = counts.shape[0]
    width = RX * GY
    f_tiles = factor_field.reshape(nfac, N_CELLS, width).transpose(1, 0, 2)
    c_tiles = counts.reshape(ncat, N_CELLS, width).transpose(1, 0, 2)
    l_tiles = land_mask.reshape(N_CELLS, width)
    e_tiles = log_exposure.reshape(N_CELLS, width)

    def scan_tile(running, tile_item):
        flat_tile, count_int, land_int, log_exp = tile_item
        count_rows = count_int.astype(jnp.float32)
        land_weight = land_int.astype(jnp.float32)
        exposure = jnp.exp(log_exp)
        mix_logit, joint_score = tile_scores(flat_tile, count_rows, exposure, profile, mixing)
        top_mix = jnp.max(mix_logit, axis=0)
        log_mix = top_mix + jnp.log(jnp.sum(jnp.exp(mix_logit - top_mix[None, :]), axis=0))
        top_joint = jnp.max(joint_score, axis=0)
        log_joint = top_joint + jnp.log(jnp.sum(jnp.exp(joint_score - top_joint[None, :]), axis=0))
        grad_counts, rate_mass, grad_mix, field_lik, log_dens = tile_grads(
            flat_tile, count_rows, land_weight, exposure, mixing, mix_logit, joint_score, log_mix, log_joint)
        running = (running[0] + grad_counts, running[1] + rate_mass, running[2] + grad_mix, running[3] + log_dens)
        return running, field_lik

    start = (jnp.zeros(profile.shape, jnp.float32), jnp.zeros((profile.shape[0],), jnp.float32),
             jnp.zeros(mixing.shape, jnp.float32), jnp.zeros((), jnp.float32))
    totals, lik_tiles = lax.scan(scan_tile, start, (f_tiles, c_tiles, l_tiles, e_tiles))
    field_lik = lik_tiles.transpose(1, 0, 2).reshape(factor_field.shape)
    land_float = land_mask.astype(jnp.float32)
    padded = jnp.pad(factor_field, ((0, 0), (1, 1), (0, 0)))
    land_pad = jnp.pad(land_float, ((1, 1), (0, 0)))
    prior_grad, prior_energy = field_prior(padded, land_pad, field_tau)
    grad_field = prior_grad + field_lik
    grad_profile = totals[0] - jnp.exp(profile) * totals[1][:, None] - 0.25 * profile
    grad_mixing = totals[2] - mixing
    log_dens = totals[3] - prior_energy - 0.125 * jnp.sum(profile * profile) - 0.5 * jnp.sum(mixing * mixing)
    return log_dens, grad_field, grad_profile, grad_mixing


def reference(factor_field, profile, mixing, factor_mom, profile_mom, mixing_mom, field_tau, counts, land_mask, log_exposure):
    step_field = 0.05
    step_profile = 0.002
    step_mixing = 0.002
    first = log_terms(factor_field, profile, mixing, counts, land_mask, log_exposure, field_tau)
    half_field = factor_mom + 0.5 * step_field * first[1]
    half_profile = profile_mom + 0.5 * step_profile * first[2]
    half_mixing = mixing_mom + 0.5 * step_mixing * first[3]
    new_field = factor_field + step_field * half_field
    new_profile = profile + step_profile * half_profile
    new_mixing = mixing + step_mixing * half_mixing
    second = log_terms(new_field, new_profile, new_mixing, counts, land_mask, log_exposure, field_tau)
    new_factor_mom = half_field + 0.5 * step_field * second[1]
    new_profile_mom = half_profile + 0.5 * step_profile * second[2]
    new_mixing_mom = half_mixing + 0.5 * step_mixing * second[3]
    kinetic = 0.5 * (jnp.sum(new_factor_mom * new_factor_mom) + jnp.sum(new_profile_mom * new_profile_mom)
                     + jnp.sum(new_mixing_mom * new_mixing_mom))
    hamiltonian = (kinetic - second[0]) / (GX * GY)
    return new_field, new_profile, new_mixing, new_factor_mom, new_profile_mom, new_mixing_mom, hamiltonian
```

```python
import jax
import jax.numpy as jnp
from jax import lax
from jax.experimental import pallas as pl
from jax.experimental.pallas import tpu as pltpu
from jax.sharding import PartitionSpec as P

F32 = jnp.float32
BF16 = jnp.bfloat16
MESH = pl.DeviceIdType.MESH
NZ = 8
NU = 8
NY = 4
ROWS = 4
WIDE = 256
FAC = 16
SLOT = 9
AHEAD = 2
BEHIND = 2


def split3(v):
    hi = v.astype(BF16)
    rest = v - hi.astype(F32)
    mid = rest.astype(BF16)
    low = (rest - mid.astype(F32)).astype(BF16)
    return hi, mid, low


def split2(v):
    hi = v.astype(BF16)
    return hi, (v - hi.astype(F32)).astype(BF16)


def dot(a, b, ca, cb, precision=None):
    return lax.dot_general(
        a, b, (((ca,), (cb,)), ((), ())), precision=precision, preferred_element_type=F32
    )


def iota(shape, dim):
    return lax.broadcasted_iota(jnp.int32, shape, dim)


def own_lanes():
    return iota((64, 128), 1) // FAC == iota((64, 128), 0) % 8


def packed_rows(wide):
    kept = jnp.where(own_lanes(), wide, 0.0)
    return kept.reshape(8, 8, 128).sum(axis=1)


def spread_rows(packed):
    wide = jnp.broadcast_to(packed[:, None, :], (8, 8, 128)).reshape(64, 128)
    return jnp.where(own_lanes(), wide, 0.0)


def lane_pick():
    return (iota((FAC, 128), 1) % FAC == iota((FAC, 128), 0)).astype(F32)


def pack_loadings(w):
    return packed_rows(dot(w, lane_pick(), 0, 0, lax.Precision.HIGHEST))


def unpack_loadings(packed):
    return dot(lane_pick(), spread_rows(packed), 1, 1, lax.Precision.HIGHEST)


def order_offset(k):
    return jnp.where(k % 2 == 1, (k + 1) // 2, (NZ - k // 2) % NZ)


def leap_kernel(
    tau_ref, f_hbm, b_hbm, w_hbm, fm_hbm, bm_hbm, wm_hbm, c_hbm, land_hbm, loge_hbm,
    nf_hbm, nb_hbm, nw_hbm, nfm_hbm, nbm_hbm, nwm_hbm, ham_hbm,
    f_v, b_v, w_v, fm_v, bm_v, wm_v, cint_v, land_v, loge_v,
    nf_v, nb_v, nw_v, nfm_v, nbm_v, nwm_v, ham_v,
    q_v, pm_v, half_v, mom_v, cbf_v, rowv_v, f128_v, ftile_v, pick_v, w128_v,
    fcur_v, hfield_v, prior_v,
    ea_v, es_v, ma_v, ms_v, run_v, gh_v, gl_v,
    sb_v, rb_v, zs_v, zr_v, yr_v, hs_v, hr_v, ls_v, lr_v, zsc_v, usc_v,
    in_sem, cnt_sem, out_sem,
    agz_s, agz_r, agu_s, agu_r, rsu_s, rsu_r, rsz_s, rsz_r, ys_s, ys_r,
    halo_s, halo_r, land_s, land_r, mom_s, mom_r, sz_s, sz_r, su_s, su_r,
):
    c = lax.axis_index("cells")
    z = lax.axis_index("comp")
    y = c // NU
    u = c % NU
    place = c * NZ + z

    def zpeer(k):
        return (c, (z + k) % NZ)

    def upeer(k):
        return (y * NU + (u + k) % NU, z)

    def ypeer(k):
        return (((y + k) % NY) * NU + u, z)

    after = (place + 1) % 256
    before = (place + 255) % 256
    nxt = (after // NZ, after % NZ)
    prv = (before // NZ, before % NZ)

    def send(src, dst, s_sem, r_sem, peer):
        pltpu.make_async_remote_copy(
            src_ref=src, dst_ref=dst, send_sem=s_sem, recv_sem=r_sem,
            device_id=peer, device_id_type=MESH,
        ).start()

    def settle(ref, sem):
        pltpu.make_async_copy(ref, ref, sem).wait()

    loads = [
        (f_hbm, f_v), (b_hbm, b_v), (w_hbm, w_v), (fm_hbm, fm_v), (bm_hbm, bm_v),
        (wm_hbm, wm_v), (land_hbm, land_v), (loge_hbm, loge_v),
    ]
    copies = [pltpu.make_async_copy(s, d, in_sem.at[i]) for i, (s, d) in enumerate(loads)]
    for cp in copies:
        cp.start()
    count_copies = [
        pltpu.make_async_copy(c_hbm.at[:, ROWS * z + r, :], cint_v.at[r], cnt_sem.at[r])
        for r in range(ROWS)
    ]
    for cp in count_copies:
        cp.start()

    barrier = pltpu.get_barrier_semaphore()
    greeted = [zpeer(k) for k in range(1, NZ)] + [upeer(k) for k in range(1, NU)]
    greeted += [ypeer(k) for k in range(1, NY)] + [nxt, prv]
    for peer in greeted:
        pl.semaphore_signal(barrier, inc=1, device_id=peer, device_id_type=MESH)

    for cp in copies:
        cp.wait()

    q_v[0, z, :, 0:8, :] = b_v[...].reshape(8, 8, 128)
    q_v[0, z, :, 8, :] = pack_loadings(w_v[...])
    pm_v[:, 0:8, :] = bm_v[...].reshape(8, 8, 128)
    pm_v[:, 8, :] = pack_loadings(wm_v[...])
    for r in range(ROWS):
        fcur_v[r] = f_v[:, r, :]
        rowv_v[0, r : r + 1, :] = land_v[pl.ds(ROWS * z + r, 1), :].astype(F32)
        rowv_v[1, r : r + 1, :] = jnp.exp(loge_v[pl.ds(ROWS * z + r, 1), :])
    hs_v[0, 0] = fcur_v[ROWS - 1]
    hs_v[0, 1] = fcur_v[0]
    ls_v[0] = rowv_v[0, ROWS - 1 : ROWS, :]
    ls_v[1] = rowv_v[0, 0:1, :]

    src_lane = iota((384, 128), 0)
    dst_lane = iota((384, 128), 1)
    part = src_lane // 128
    group = dst_lane // FAC
    first = (part == 0) & ((group == 0) | (group == 3) | (group == 5))
    second = (part == 1) & ((group == 1) | (group == 4))
    third = (part == 2) & (group == 2)
    same = src_lane % FAC == dst_lane % FAC
    pick_v[...] = jnp.where(same & (first | second | third), 1.0, 0.0).astype(BF16)

    tau = jnp.zeros((FAC, WIDE), F32)
    fac_row = iota((FAC, WIDE), 0)
    for j in range(FAC):
        tau = jnp.where(fac_row == j, tau_ref[j], tau)

    pl.semaphore_wait(barrier, len(greeted))

    def gather_start(ev):
        mine = q_v.at[ev, z, u, pl.ds(0, SLOT), :]
        for k in (1, 7, 2, 6, 3, 5, 4):
            send(mine, mine, agz_s.at[ev], agz_r.at[ev, z], zpeer(k))

    def gather_forward(ev, g):
        piece = q_v.at[ev, g, u, pl.ds(0, SLOT), :]
        for k in range(1, NU):
            send(piece, piece, agu_s.at[ev, g], agu_r.at[ev, g], upeer(k))

    def seven(ref, rows=SLOT):
        return ref.at[pl.ds(0, 7), pl.ds(0, rows), :]

    def halo_start(ev):
        send(hs_v.at[ev, 0], hr_v.at[ev, 0], halo_s.at[ev, 0], halo_r.at[ev, 0], nxt)
        send(hs_v.at[ev, 1], hr_v.at[ev, 1], halo_s.at[ev, 1], halo_r.at[ev, 1], prv)

    def field_pieces():
        for r in range(ROWS):
            hi, mid, low = split3(fcur_v[r])
            none = jnp.zeros((FAC, WIDE), BF16)
            f128_v[r] = jnp.concatenate([hi, hi, hi, mid, mid, low, none, none], axis=0)
            ftile_v[r] = jnp.concatenate([hi] * 8 + [mid] * 8, axis=0)

    def prior(ev):
        settle(hr_v.at[ev, 0], halo_r.at[ev, 0])
        settle(hr_v.at[ev, 1], halo_r.at[ev, 1])
        if ev == 0:
            settle(lr_v.at[0], land_r.at[0])
            settle(lr_v.at[1], land_r.at[1])
        land_prev = jnp.where(place > 0, lr_v[0], 0.0)
        land_next = jnp.where(place < 255, lr_v[1], 0.0)
        fields = [hr_v[ev, 0]] + [fcur_v[r] for r in range(ROWS)] + [hr_v[ev, 1]]
        lands = [land_prev] + [rowv_v[0, r : r + 1, :] for r in range(ROWS)] + [land_next]
        steps = [fields[i + 1] - fields[i] for i in range(ROWS + 1)]
        flux = [(lands[i + 1] * lands[i]) * steps[i] for i in range(ROWS + 1)]
        energy = jnp.zeros((FAC, WIDE), F32)
        lane = iota((1, WIDE), 1)
        for r in range(ROWS):
            centre, land = fields[r + 1], lands[r + 1]
            step_y = pltpu.roll(centre, WIDE - 1, 1) - centre
            edge_y = jnp.where(lane < WIDE - 1, pltpu.roll(land, WIDE - 1, 1) * land, 0.0)
            flux_y = edge_y * step_y
            back = jnp.where(lane > 0, pltpu.roll(flux_y, 1, 1), 0.0)
            lap = (flux[r] - flux[r + 1]) + (back - flux_y)
            prior_v[r] = -tau * (lap + 0.1 * centre)
            energy = energy + (
                flux[r + 1] * steps[r + 1] + flux_y * step_y + 0.1 * (centre * centre)
            )
        return 0.5 * jnp.sum(tau * energy)

    def forward(ev, k, g):
        b = q_v[ev, g, :, 0:8, :].reshape(64, 128)
        wide = spread_rows(q_v[ev, g, :, 8, :])
        stacked = jnp.concatenate(split3(b), axis=0)
        w128 = dot(jnp.concatenate(split3(wide), axis=1), pick_v[...], 1, 0).astype(BF16)
        w128_v[pl.ds(pl.multiple_of(k * 64, 64), 64), :] = w128
        rate = jnp.sum(jnp.exp(b), axis=1, keepdims=True)
        for r in range(ROWS):
            a = dot(w128, f128_v[r], 1, 0)
            d = dot(stacked, cbf_v[r], 1, 0)
            s = a + (((d[128:192] + d[64:128]) + d[0:64]) - rate * rowv_v[1, r : r + 1, :])
            for i, (v, e_ref, m_ref) in enumerate(((a, ea_v, ma_v), (s, es_v, ms_v))):
                top = jnp.max(v, axis=0, keepdims=True)
                e = jnp.exp(v - top)
                e_ref[k, r] = e
                m_ref[k, r : r + 1, :] = top
                run = run_v[2 * i, r : r + 1, :]
                new = jnp.maximum(run, top)
                run_v[2 * i + 1, r : r + 1, :] = run_v[2 * i + 1, r : r + 1, :] * jnp.exp(
                    run - new
                ) + jnp.sum(e, axis=0, keepdims=True) * jnp.exp(top - new)
                run_v[2 * i, r : r + 1, :] = new

    def group_of(k):
        return (z + order_offset(k)) % NZ

    def arrive_and_forward(ev, k):
        g = group_of(k)
        settle(q_v.at[ev, g, u, pl.ds(0, SLOT), :], agz_r.at[ev, g])
        gather_forward(ev, g)

    def forward_all(ev):
        run_v[0] = jnp.full((8, WIDE), -3e38, F32)
        run_v[1] = jnp.zeros((8, WIDE), F32)
        run_v[2] = jnp.full((8, WIDE), -3e38, F32)
        run_v[3] = jnp.zeros((8, WIDE), F32)
        if ev == 0:
            forward(ev, 0, z)
        for k in range(1, 1 + AHEAD):
            arrive_and_forward(ev, jnp.int32(k))

        def step(k, carry):
            @pl.when(k + AHEAD < NZ)
            def _():
                arrive_and_forward(ev, k + AHEAD)

            g = group_of(k)
            settle(seven(q_v.at[ev, g]), agu_r.at[ev, g])
            forward(ev, k, g)
            return carry

        if ev == 1:
            settle(seven(q_v.at[ev, z]), agu_r.at[ev, z])
            forward(ev, 0, z)
        lax.fori_loop(1, NZ, step, 0)

    def reduce_group(ev, g):
        settle(seven(rb_v.at[ev, g]), rsu_r.at[ev, g])
        acc = sb_v[ev, g, u, 0:SLOT, :]
        for j in range(7):
            acc = acc + rb_v[ev, g, j, 0:SLOT, :]
        return acc

    def pass_on(ev, k):
        g = group_of(k)
        zs_v[ev, g, 0:SLOT, :] = reduce_group(ev, g)
        slot = (g + NZ - z) % NZ - 1
        send(
            zs_v.at[ev, g, pl.ds(0, SLOT), :], zr_v.at[ev, slot, pl.ds(0, SLOT), :],
            rsz_s.at[ev], rsz_r.at[ev], (c, g),
        )

    def backward_all(ev):
        for r in range(ROWS):
            land = rowv_v[0, r : r + 1, :]
            run_v[1, r : r + 1, :] = land / run_v[1, r : r + 1, :]
            run_v[3, r : r + 1, :] = land / run_v[3, r : r + 1, :]

        def step(i, carry):
            k = NZ - 1 - i
            g = group_of(k)
            b = q_v[ev, g, :, 0:8, :].reshape(64, 128)
            gc = jnp.zeros((128, 128), F32)
            gw = jnp.zeros((128, 256), F32)
            mass = jnp.zeros((64, WIDE), F32)
            for r in range(ROWS):
                top_a = run_v[0, r : r + 1, :]
                top_s = run_v[2, r : r + 1, :]
                scale_a = jnp.exp(ma_v[k, r : r + 1, :] - top_a) * run_v[1, r : r + 1, :]
                scale_s = jnp.exp(ms_v[k, r : r + 1, :] - top_s) * run_v[3, r : r + 1, :]
                p = es_v[k, r] * scale_s
                gap = p - ea_v[k, r] * scale_a
                gc = gc + dot(jnp.concatenate(split2(p), axis=0), cbf_v[r], 1, 1)
                mass = mass + p * rowv_v[1, r : r + 1, :]
                hi, low = split2(gap)
                gw = gw + dot(jnp.concatenate([hi, low], axis=0), ftile_v[r], 1, 1)
                at = pl.ds(pl.multiple_of(k * 64, 64), 64)
                gh_v[r, at, :] = hi
                gl_v[r, at, :] = low
            rate_mass = jnp.sum(mass, axis=1, keepdims=True)
            gb = (gc[0:64] + gc[64:128]) - jnp.exp(b) * rate_mass
            wide = (gw[64:128, 128:256] + gw[64:128, 0:128]) + gw[0:64, 128:256]
            sb_v[ev, g, :, 0:8, :] = gb.reshape(8, 8, 128)
            sb_v[ev, g, :, 8, :] = packed_rows(wide + gw[0:64, 0:128])
            for j in range(1, NU):
                send(
                    sb_v.at[ev, g, (u + j) % NU, pl.ds(0, SLOT), :],
                    rb_v.at[ev, g, j - 1, pl.ds(0, SLOT), :],
                    rsu_s.at[ev, g], rsu_r.at[ev, g], upeer(j),
                )

            @pl.when(i >= BEHIND)
            def _():
                pass_on(ev, NZ - 1 - (i - BEHIND))

            return carry

        lax.fori_loop(0, NZ, step, 0)
        for i in range(NZ - BEHIND, NZ - 1):
            pass_on(ev, jnp.int32(NZ - 1 - i))

    def field_lik(r):
        both = dot(w128_v[...], gh_v[r], 0, 0) + dot(w128_v[...], gl_v[r], 0, 0)
        return (both[32:48] + both[16:32]) + both[0:16]

    def piece_total(ev, extra):
        own = reduce_group(ev, z)
        settle(seven(zr_v.at[ev]), rsz_r.at[ev])
        for j in range(7):
            own = own + zr_v[ev, j, 0:SLOT, :]
        yr_v[ev, y, 0:SLOT, :] = own
        yr_v[ev, y, SLOT : SLOT + 1, :] = jnp.full((1, 128), extra, F32)
        mine = yr_v.at[ev, y, pl.ds(0, SLOT + 1), :]
        for k in range(1, NY):
            send(mine, mine, ys_s.at[ev], ys_r.at[ev], ypeer(k))

    def piece_sum(ev):
        settle(yr_v.at[ev, pl.ds(0, NY - 1), pl.ds(0, SLOT + 1), :], ys_r.at[ev])
        total = yr_v[ev, 0, 0 : SLOT + 1, :]
        for k in range(1, NY):
            total = total + yr_v[ev, k, 0 : SLOT + 1, :]
        return total[0:SLOT], total[SLOT : SLOT + 1]

    gather_start(0)
    halo_start(0)
    send(ls_v.at[0], lr_v.at[0], land_s.at[0], land_r.at[0], nxt)
    send(ls_v.at[1], lr_v.at[1], land_s.at[1], land_r.at[1], prv)
    field_pieces()
    for r in range(ROWS):
        count_copies[r].wait()
        cbf_v[r] = cint_v[r].astype(F32).astype(BF16)
    forward_all(0)
    prior(0)
    backward_all(0)

    piece_total(0, jnp.float32(0.0))
    for r in range(ROWS):
        half = fm_v[:, r, :] + 0.025 * (prior_v[r] + field_lik(r))
        hfield_v[r] = half
        new = fcur_v[r] + 0.05 * half
        fcur_v[r] = new
        nf_v[:, r, :] = new
    hs_v[1, 0] = fcur_v[ROWS - 1]
    hs_v[1, 1] = fcur_v[0]
    halo_start(1)

    pull = jnp.where(iota((SLOT, 128), 0) < 8, 0.25, 1.0)
    lik, _ = piece_sum(0)
    q0 = q_v[0, z, u, 0:SLOT, :]
    half_q = pm_v[u, 0:SLOT, :] + 0.001 * (lik - pull * q0)
    q1 = q0 + 0.002 * half_q
    half_v[0:SLOT, :] = half_q
    q_v[1, z, u, 0:SLOT, :] = q1
    gather_start(1)
    gather_forward(1, z)
    out_nf = pltpu.make_async_copy(nf_v, nf_hbm, out_sem.at[0])
    out_nf.start()
    field_pieces()
    energy = prior(1)
    forward_all(1)
    log_dens = jnp.zeros((1, WIDE), F32)
    for r in range(ROWS):
        log_mix = run_v[0, r : r + 1, :] + jnp.log(run_v[1, r : r + 1, :])
        log_joint = run_v[2, r : r + 1, :] + jnp.log(run_v[3, r : r + 1, :])
        log_dens = log_dens + rowv_v[0, r : r + 1, :] * (log_joint - log_mix)
    log_part = jnp.sum(log_dens) - energy
    backward_all(1)
    nb_v[...] = q_v[1, z, :, 0:8, :].reshape(64, 128)
    nw_v[...] = unpack_loadings(q_v[1, z, :, 8, :])
    out_nb = pltpu.make_async_copy(nb_v, nb_hbm, out_sem.at[1])
    out_nw = pltpu.make_async_copy(nw_v, nw_hbm, out_sem.at[2])
    out_nb.start()
    out_nw.start()
    square = jnp.zeros((FAC, WIDE), F32)
    for r in range(ROWS):
        last = hfield_v[r] + 0.025 * (prior_v[r] + field_lik(r))
        nfm_v[:, r, :] = last
        square = square + last * last
    out_nfm = pltpu.make_async_copy(nfm_v, nfm_hbm, out_sem.at[3])
    out_nfm.start()
    piece_total(1, 0.5 * jnp.sum(square) - log_part)
    lik, part_sum = piece_sum(1)
    q1 = q_v[1, z, u, 0:SLOT, :]
    mom = half_v[0:SLOT, :] + 0.001 * (lik - pull * q1)
    mom_v[u, 0:SLOT, :] = mom
    weight = 0.5 * pull
    scalar = part_sum + jnp.sum(0.5 * (mom * mom) + weight * (q1 * q1))
    zsc_v[z] = scalar
    for k in (4, 3, 5, 2, 6, 1, 7):
        send(zsc_v.at[z], zsc_v.at[z], sz_s, sz_r, zpeer(k))
    mine = mom_v.at[u, pl.ds(0, SLOT), :]
    for k in range(1, NU):
        send(mine, mine, mom_s, mom_r, upeer(k))
    settle(zsc_v.at[pl.ds(0, 7)], sz_r)
    total = zsc_v[0]
    for k in range(1, NZ):
        total = total + zsc_v[k]
    usc_v[u] = total
    for k in range(1, NU):
        send(usc_v.at[u], usc_v.at[u], su_s, su_r, upeer(k))
    settle(seven(mom_v), mom_r)
    nbm_v[...] = mom_v[:, 0:8, :].reshape(64, 128)
    nwm_v[...] = unpack_loadings(mom_v[:, 8, :])
    out_nbm = pltpu.make_async_copy(nbm_v, nbm_hbm, out_sem.at[4])
    out_nwm = pltpu.make_async_copy(nwm_v, nwm_hbm, out_sem.at[5])
    out_nbm.start()
    out_nwm.start()
    settle(usc_v.at[pl.ds(0, 7)], su_r)
    total = usc_v[0]
    for k in range(1, NU):
        total = total + usc_v[k]
    ham_v[...] = total * (1.0 / 262144.0)
    out_ham = pltpu.make_async_copy(ham_v, ham_hbm, out_sem.at[6])
    out_ham.start()

    for ev in range(2):
        settle(seven(q_v.at[ev, z]), agz_s.at[ev])
        settle(seven(zs_v.at[ev]), rsz_s.at[ev])
        settle(yr_v.at[ev, pl.ds(0, NY - 1), pl.ds(0, SLOT + 1), :], ys_s.at[ev])
        for i in range(2):
            settle(hs_v.at[ev, i], halo_s.at[ev, i])

        def drained(k, carry):
            g = (z + k) % NZ
            settle(seven(q_v.at[ev, g]), agu_s.at[ev, g])
            return carry

        lax.fori_loop(1 - ev, NZ, drained, 0)

        def sent(g, carry):
            settle(seven(sb_v.at[ev, g]), rsu_s.at[ev, g])
            return carry

        lax.fori_loop(0, NZ, sent, 0)
    settle(ls_v.at[0], land_s.at[0])
    settle(ls_v.at[1], land_s.at[1])
    settle(zsc_v.at[pl.ds(0, 7)], sz_s)
    settle(usc_v.at[pl.ds(0, 7)], su_s)
    settle(seven(mom_v), mom_s)
    for out in (out_nf, out_nb, out_nw, out_nfm, out_nbm, out_nwm, out_ham):
        out.wait()


def per_device(
    factor_field, profile, mixing, factor_mom, profile_mom, mixing_mom, field_tau,
    counts, land_mask, log_exposure,
):
    hbm = pl.BlockSpec(memory_space=pltpu.MemorySpace.HBM)
    vm = pltpu.VMEM
    dma = pltpu.SemaphoreType.DMA
    shapes = [
        jax.ShapeDtypeStruct(a.shape, F32)
        for a in (factor_field, profile, mixing, factor_mom, profile_mom, mixing_mom)
    ]
    shapes.append(jax.ShapeDtypeStruct((1, 128), F32))
    scratch = [
        vm((FAC, ROWS, WIDE), F32), vm((64, 128), F32), vm((FAC, 64), F32),
        vm((FAC, ROWS, WIDE), F32), vm((64, 128), F32), vm((FAC, 64), F32),
        vm((ROWS, 128, WIDE), jnp.int32), vm((32, WIDE), jnp.int32), vm((32, WIDE), F32),
        vm((FAC, ROWS, WIDE), F32), vm((64, 128), F32), vm((FAC, 64), F32),
        vm((FAC, ROWS, WIDE), F32), vm((64, 128), F32), vm((FAC, 64), F32), vm((1, 128), F32),
        vm((2, NZ, NU, 16, 128), F32), vm((NU, 16, 128), F32), vm((16, 128), F32),
        vm((NU, 16, 128), F32), vm((ROWS, 128, WIDE), BF16), vm((2, 8, WIDE), F32),
        vm((ROWS, 128, WIDE), BF16), vm((ROWS, 256, WIDE), BF16), vm((384, 128), BF16),
        vm((512, 128), BF16),
        vm((ROWS, FAC, WIDE), F32), vm((ROWS, FAC, WIDE), F32), vm((ROWS, FAC, WIDE), F32),
        vm((NZ, ROWS, 64, WIDE), F32), vm((NZ, ROWS, 64, WIDE), F32),
        vm((NZ, 8, WIDE), F32), vm((NZ, 8, WIDE), F32), vm((4, 8, WIDE), F32),
        vm((ROWS, 512, WIDE), BF16), vm((ROWS, 512, WIDE), BF16),
        vm((2, NZ, NU, 16, 128), F32), vm((2, NZ, NU, 16, 128), F32),
        vm((2, NZ, 16, 128), F32), vm((2, NZ, 16, 128), F32), vm((2, NY, 16, 128), F32),
        vm((2, 2, FAC, WIDE), F32), vm((2, 2, FAC, WIDE), F32),
        vm((2, 1, WIDE), F32), vm((2, 1, WIDE), F32), vm((NZ, 1, 128), F32), vm((NU, 1, 128), F32),
        dma((8,)), dma((ROWS,)), dma((7,)),
        dma((2,)), dma((2, NZ)), dma((2, NZ)), dma((2, NZ)), dma((2, NZ)), dma((2, NZ)),
        dma((2,)), dma((2,)), dma((2,)), dma((2,)),
        dma((2, 2)), dma((2, 2)), dma((2,)), dma((2,)), dma, dma, dma, dma, dma, dma,
    ]
    outs = pl.pallas_call(
        leap_kernel,
        out_shape=shapes,
        in_specs=[pl.BlockSpec(memory_space=pltpu.MemorySpace.SMEM)] + [hbm] * 9,
        out_specs=[hbm] * 7,
        scratch_shapes=scratch,
        compiler_params=pltpu.CompilerParams(
            collective_id=0, has_side_effects=True, vmem_limit_bytes=56 * 1024 * 1024
        ),
        name="leapfrog",
    )(
        field_tau, factor_field, profile, mixing, factor_mom, profile_mom, mixing_mom,
        counts, land_mask, log_exposure,
    )
    return (*outs[:6], outs[6][0, 0])


def solution(mesh):
    rows = P(None, ("cells", "comp"), None)
    ins = (
        rows, P("comp", None), P(None, "comp"), rows, P("comp", None), P(None, "comp"),
        P(), P(None, "cells", None), P("cells", None), P("cells", None),
    )
    outs = (
        rows, P("comp", None), P(None, "comp"), rows, P("comp", None), P(None, "comp"), P(),
    )
    return jax.shard_map(per_device, mesh=mesh, in_specs=ins, out_specs=outs, check_vma=False)
```

```python
import jax
import jax.numpy as jnp
from jax import lax
from jax.experimental import pallas as pl
from jax.experimental.pallas import tpu as pltpu
from jax.sharding import PartitionSpec as P

F32 = jnp.float32
BF16 = jnp.bfloat16
MESH = pl.DeviceIdType.MESH
NZ = 8
NQ = 16
NC = 32
ROWS = 4
WIDE = 256
FAC = 16
SLOT = 9
LOG2E = 1.4426950408889634
LN2 = 0.6931471805599453


def split3(v):
    hi = v.astype(BF16)
    rest = v - hi.astype(F32)
    mid = rest.astype(BF16)
    low = (rest - mid.astype(F32)).astype(BF16)
    return hi, mid, low


def split2(v):
    hi = v.astype(BF16)
    return hi, (v - hi.astype(F32)).astype(BF16)


def dot(a, b, ca, cb, precision=None):
    return lax.dot_general(
        a, b, (((ca,), (cb,)), ((), ())), precision=precision, preferred_element_type=F32
    )


def iota(shape, dim):
    return lax.broadcasted_iota(jnp.int32, shape, dim)


def own_lanes(rows):
    return iota((rows, 128), 1) // FAC == iota((rows, 128), 0) % 8


def packed_rows(wide):
    rows = wide.shape[0]
    kept = jnp.where(own_lanes(rows), wide, 0.0)
    return kept.reshape(rows // 8, 8, 128).sum(axis=1)


def spread_rows(packed):
    groups = packed.shape[0]
    wide = jnp.broadcast_to(packed[:, None, :], (groups, 8, 128)).reshape(groups * 8, 128)
    return jnp.where(own_lanes(groups * 8), wide, 0.0)


def lane_pick():
    return (iota((FAC, 128), 1) % FAC == iota((FAC, 128), 0)).astype(F32)


def pack_loadings(w):
    return packed_rows(dot(w, lane_pick(), 0, 0, lax.Precision.HIGHEST))


def unpack_loadings(packed):
    return dot(lane_pick(), spread_rows(packed), 1, 1, lax.Precision.HIGHEST)


def leap_kernel(
    tau_ref, f_hbm, b_hbm, w_hbm, fm_hbm, bm_hbm, wm_hbm, c_hbm, land_hbm, loge_hbm,
    nf_v, nb_v, nw_v, nfm_v, nbm_v, nwm_v, ham_v,
    f_v, b_v, w_v, fm_v, bm_v, wm_v, cint_v, land_v, loge_v,
    q_v, pm_v, mp_v, half_v, mo_v, cx_v, ks_v, rowv_v, ftile_v, pick_v, w128_v,
    fcur_v, hfield_v, prior_v, ea_v, es_v, ma_v, ms_v, run_v, gh_v, gl_v,
    sb_v, cb_v, xr_v, zb_v, hs_v, hr_v, ls_v, lr_v, sc_v, tally_v,
    in_sem, cnt_sem, ag_s, ag_r, fw_s, mp_s, mp_r, cb_s, cb_r, x_s, x_r, zb_s, zb_r,
    s3_s, s3_r, f3_s, f3_r, halo_s, halo_r, land_s, land_r, sc_s, sc_r, mo_s, mo_r,
):
    c = lax.axis_index("cells")
    z = lax.axis_index("comp")
    y = c // 8
    x = (c % 8) // 2
    core = c % 2
    chip = c // 2
    place = c * NZ + z
    zc = z // 2
    near = core == z // 4
    far_order = (4, 3, 5, 2, 6, 1, 7)
    partner = (2 * chip + 1 - core, z)

    def zpeer(k):
        return (c, (z + k) % NZ)

    turns = sorted(
        ((a, b) for a in range(4) for b in range(4) if a or b),
        key=lambda t: -(min(t[0], 4 - t[0]) + min(t[1], 4 - t[1])),
    )

    def chip_at(a, b):
        return ((y + a) % 4) * 4 + (x + b) % 4

    after = (place + 1) % 256
    before = (place + 255) % 256
    nxt = (after // NZ, after % NZ)
    prv = (before // NZ, before % NZ)

    def send(src, dst, s_sem, r_sem, peer):
        pltpu.make_async_remote_copy(
            src_ref=src, dst_ref=dst, send_sem=s_sem, recv_sem=r_sem,
            device_id=peer, device_id_type=MESH,
        ).start()

    def settle(ref, sem):
        pltpu.make_async_copy(ref, ref, sem).wait()

    loads = [
        (f_hbm, f_v), (b_hbm, b_v), (w_hbm, w_v), (fm_hbm, fm_v), (bm_hbm, bm_v),
        (wm_hbm, wm_v), (land_hbm, land_v), (loge_hbm, loge_v),
    ]
    copies = [pltpu.make_async_copy(s, d, in_sem.at[i]) for i, (s, d) in enumerate(loads)]
    for cp in copies:
        cp.start()
    count_copies = [
        pltpu.make_async_copy(c_hbm.at[:, ROWS * z + r, :], cint_v.at[r], cnt_sem.at[r])
        for r in range(ROWS)
    ]
    for cp in count_copies:
        cp.start()

    barrier = pltpu.get_barrier_semaphore()
    greeted = [zpeer(k) for k in far_order] + [((c + k) % NC, z) for k in range(1, NC)]
    greeted += [nxt, prv]
    for peer in greeted:
        pl.semaphore_signal(barrier, inc=1, device_id=peer, device_id_type=MESH)

    for cp in copies:
        cp.wait()

    half = pl.ds(pl.multiple_of((z % 2) * 8, 8), 8)
    q_v[0, zc, half, 0:8, :] = b_v[...].reshape(8, 8, 128)
    q_v[0, zc, half, 8, :] = pack_loadings(w_v[...])
    pm_v[:, 0:8, :] = bm_v[...].reshape(8, 8, 128)
    pm_v[:, 8, :] = pack_loadings(wm_v[...])
    for r in range(ROWS):
        fcur_v[r] = f_v[:, r, :]
        rowv_v[0, r : r + 1, :] = land_v[pl.ds(ROWS * z + r, 1), :].astype(F32)
        rowv_v[1, r : r + 1, :] = jnp.exp(loge_v[pl.ds(ROWS * z + r, 1), :])
    hs_v[0, 0] = fcur_v[ROWS - 1]
    hs_v[0, 1] = fcur_v[0]
    ls_v[0] = rowv_v[0, ROWS - 1 : ROWS, :]
    ls_v[1] = rowv_v[0, 0:1, :]

    src_lane = iota((384, 128), 0)
    dst_lane = iota((384, 128), 1)
    part = src_lane // 128
    group = dst_lane // FAC
    first = (part == 0) & ((group == 0) | (group == 3) | (group == 5))
    second = (part == 1) & ((group == 1) | (group == 4))
    third = (part == 2) & (group == 2)
    same = src_lane % FAC == dst_lane % FAC
    pick_v[...] = jnp.where(same & (first | second | third), 1.0, 0.0).astype(BF16)

    tau = jnp.zeros((FAC, WIDE), F32)
    fac_row = iota((FAC, WIDE), 0)
    for j in range(FAC):
        tau = jnp.where(fac_row == j, tau_ref[j], tau)

    pl.semaphore_wait(barrier, len(greeted))

    def shard(g):
        rows = pl.ds(pl.multiple_of((g % 2) * 8, 8), 8)
        return q_v.at[0, g // 2, rows, pl.ds(0, SLOT), :]

    @pl.when(near)
    def _():
        for k in far_order:
            send(shard(z), shard(z), ag_s, ag_r.at[z], zpeer(k))

    send(hs_v.at[0, 0], hr_v.at[0, 0], halo_s.at[0, 0], halo_r.at[0, 0], nxt)
    send(hs_v.at[0, 1], hr_v.at[0, 1], halo_s.at[0, 1], halo_r.at[0, 1], prv)
    send(ls_v.at[0], lr_v.at[0], land_s.at[0], land_r.at[0], nxt)
    send(ls_v.at[1], lr_v.at[1], land_s.at[1], land_r.at[1], prv)
    mom_owner = near & (z % 2 == chip // 8)
    mom_slot = (z % 4) // 2

    @pl.when(mom_owner)
    def _():
        mp_v[mom_slot, 0:SLOT, :] = pm_v[chip % 8, 0:SLOT, :]
        for k in far_order:
            send(
                pm_v.at[chip % 8, pl.ds(0, SLOT), :], mp_v.at[mom_slot, pl.ds(0, SLOT), :],
                mp_s, mp_r.at[mom_slot], zpeer(k),
            )

    def expand(parts, shape):
        row = iota(shape, 0)
        out = jnp.zeros(shape, F32)
        for i, v in enumerate(parts):
            out = jnp.where(row == i, v.astype(F32), out)
        return out.astype(BF16)

    def field_pieces():
        for r in range(ROWS):
            hi, mid, low = split3(fcur_v[r])
            e_hi, e_mid, e_low = split3(rowv_v[1, r : r + 1, :])
            shares = expand((e_hi, e_mid, e_low, e_hi, e_mid, e_hi), (FAC, WIDE))
            none = jnp.zeros((FAC, WIDE), BF16)
            ks_v[r, 0:128, :] = jnp.concatenate(
                [hi, hi, hi, mid, mid, low, shares, none], axis=0
            )
            ftile_v[r] = jnp.concatenate([hi] * 8 + [mid] * 8, axis=0)

    def prior(ev):
        settle(hr_v.at[ev, 0], halo_r.at[ev, 0])
        settle(hr_v.at[ev, 1], halo_r.at[ev, 1])
        if ev == 0:
            settle(lr_v.at[0], land_r.at[0])
            settle(lr_v.at[1], land_r.at[1])
        land_prev = jnp.where(place > 0, lr_v[0], 0.0)
        land_next = jnp.where(place < 255, lr_v[1], 0.0)
        fields = [hr_v[ev, 0]] + [fcur_v[r] for r in range(ROWS)] + [hr_v[ev, 1]]
        lands = [land_prev] + [rowv_v[0, r : r + 1, :] for r in range(ROWS)] + [land_next]
        steps = [fields[i + 1] - fields[i] for i in range(ROWS + 1)]
        flux = [(lands[i + 1] * lands[i]) * steps[i] for i in range(ROWS + 1)]
        energy = jnp.zeros((FAC, WIDE), F32)
        lane = iota((1, WIDE), 1)
        for r in range(ROWS):
            centre, land = fields[r + 1], lands[r + 1]
            step_y = pltpu.roll(centre, WIDE - 1, 1) - centre
            edge_y = jnp.where(lane < WIDE - 1, pltpu.roll(land, WIDE - 1, 1) * land, 0.0)
            flux_y = edge_y * step_y
            back = jnp.where(lane > 0, pltpu.roll(flux_y, 1, 1), 0.0)
            lap = (flux[r] - flux[r + 1]) + (back - flux_y)
            prior_v[r] = -tau * (lap + 0.1 * centre)
            energy = energy + (
                flux[r + 1] * steps[r + 1] + flux_y * step_y + 0.1 * (centre * centre)
            )
        return 0.5 * jnp.sum(tau * energy)

    def forward(ev, i):
        b = q_v[ev, i, :, 0:8, :].reshape(128, 128)
        wide = spread_rows(q_v[ev, i, :, 8, :])
        spread = dot(jnp.concatenate(split3(wide * LOG2E), axis=1), pick_v[...], 1, 0)
        rate = jnp.sum(jnp.exp(b), axis=1, keepdims=True) * (-LOG2E)
        r_hi, r_mid, r_low = [v.astype(F32) for v in split3(rate)]
        lane = iota((128, 128), 1)
        shares = jnp.where(
            (lane >= 96) & (lane < 99), r_hi,
            jnp.where((lane == 99) | (lane == 100), r_mid, jnp.where(lane == 101, r_low, 0.0)),
        )
        w128 = spread.astype(BF16)
        w128_v[pl.ds(pl.multiple_of(i * 128, 128), 128), :] = w128
        lhs = jnp.concatenate(
            [(spread + shares).astype(BF16)] + list(split3(b * LOG2E)), axis=1
        )
        for r in range(ROWS):
            a = dot(w128, ks_v[r, 0:128, :], 1, 0)
            s = dot(lhs, ks_v[r], 1, 0)
            for j, (v, e_ref, m_ref) in enumerate(((a, ea_v, ma_v), (s, es_v, ms_v))):
                top = jnp.max(v, axis=0, keepdims=True)
                e = jnp.exp2(v - top)
                e_ref[i, r] = e
                m_ref[i, r : r + 1, :] = top
                run = run_v[2 * j, r : r + 1, :]
                new = jnp.maximum(run, top)
                run_v[2 * j + 1, r : r + 1, :] = run_v[2 * j + 1, r : r + 1, :] * jnp.exp2(
                    run - new
                ) + jnp.sum(e, axis=0, keepdims=True) * jnp.exp2(top - new)
                run_v[2 * j, r : r + 1, :] = new

    def chunk_of(k, a):
        base = jnp.where(k < 2, a, 3 - a)
        return jnp.where(k % 2 == 0, base, base + 1 - 2 * (base % 2))

    def clear_runs():
        run_v[0] = jnp.full((8, WIDE), -3e38, F32)
        run_v[1] = jnp.zeros((8, WIDE), F32)
        run_v[2] = jnp.full((8, WIDE), -3e38, F32)
        run_v[3] = jnp.zeros((8, WIDE), F32)

    def own_set(ev):
        return q_v.at[ev, pl.ds(2 * core, 2), :, pl.ds(0, SLOT), :]

    def forward_first():
        clear_runs()
        a = jnp.where(near, zc, 3 - zc)

        def step(k, carry):
            i = chunk_of(k, a)
            for h in range(2):
                g = 2 * i + h

                @pl.when(g != z)
                def _():
                    settle(shard(g), ag_r.at[g])

                    @pl.when(k < 2)
                    def _():
                        send(shard(g), shard(g), fw_s.at[g], ag_r.at[g], partner)

            forward(0, i)
            return carry

        lax.fori_loop(0, 4, step, 0)

    def forward_second():
        clear_runs()

        def step(k, carry):
            @pl.when(k == 2)
            def _():
                settle(own_set(1), f3_r)

            forward(1, chunk_of(k, 2 * core))
            return carry

        lax.fori_loop(0, 4, step, 0)

    def backward(ev, i):
        b = q_v[ev, i, :, 0:8, :].reshape(128, 128)
        gc = jnp.zeros((256, 256), F32)
        gw = jnp.zeros((256, 256), F32)
        for r in range(ROWS):
            top_a = run_v[0, r : r + 1, :]
            top_s = run_v[2, r : r + 1, :]
            scale_a = jnp.exp2(ma_v[i, r : r + 1, :] - top_a) * run_v[1, r : r + 1, :]
            scale_s = jnp.exp2(ms_v[i, r : r + 1, :] - top_s) * run_v[3, r : r + 1, :]
            p = es_v[i, r] * scale_s
            gap = p - ea_v[i, r] * scale_a
            gc = gc + dot(jnp.concatenate(split2(p), axis=0), cx_v[r], 1, 1)
            hi, low = split2(gap)
            gw = gw + dot(jnp.concatenate([hi, low], axis=0), ftile_v[r], 1, 1)
            at = pl.ds(pl.multiple_of(i * 128, 128), 128)
            gh_v[r, at, :] = hi
            gl_v[r, at, :] = low
        both = gc[0:128] + gc[128:256]
        rate_mass = jnp.sum(both[:, 128:256], axis=1, keepdims=True)
        gb = both[:, 0:128] - jnp.exp(b) * rate_mass
        wide = (gw[128:256, 128:256] + gw[128:256, 0:128]) + gw[0:128, 128:256]
        sb_v[ev, i, :, 0:8, :] = gb.reshape(16, 8, 128)
        sb_v[ev, i, :, 8, :] = packed_rows(wide + gw[0:128, 0:128])

    def backward_all(ev):
        for r in range(ROWS):
            land = rowv_v[0, r : r + 1, :]
            run_v[1, r : r + 1, :] = land / run_v[1, r : r + 1, :]
            run_v[3, r : r + 1, :] = land / run_v[3, r : r + 1, :]

        def step(k, carry):
            i = jnp.where(k < 2, 2 * (1 - core) + k, 2 * core + k - 2)
            backward(ev, i)

            @pl.when(k < 2)
            def _():
                send(
                    sb_v.at[ev, i, :, pl.ds(0, SLOT), :], cb_v.at[ev, k, :, pl.ds(0, SLOT), :],
                    cb_s.at[ev, k], cb_r.at[ev, k], partner,
                )

            @pl.when(k >= 2)
            def _():
                n = k - 2
                settle(cb_v.at[ev, n, :, pl.ds(0, SLOT), :], cb_r.at[ev, n])
                for q in range(NQ):
                    sb_v[ev, i, q, 0:SLOT, :] = (
                        sb_v[ev, i, q, 0:SLOT, :] + cb_v[ev, n, q, 0:SLOT, :]
                    )
                for t in turns:
                    to = chip_at(*t)
                    send(
                        sb_v.at[ev, i, to, pl.ds(0, SLOT), :],
                        xr_v.at[ev, n, chip, pl.ds(0, SLOT), :],
                        x_s.at[ev, n], x_r.at[ev, n], (2 * to + core, z),
                    )

            return carry

        lax.fori_loop(0, 4, step, 0)

    def field_lik(r):
        both = dot(w128_v[...], gh_v[r], 0, 0) + dot(w128_v[...], gl_v[r], 0, 0)
        return ((both[32:48] + both[16:32]) + both[0:16]) * LN2

    def fifteen(ref):
        return ref.at[pl.ds(0, NQ - 1), pl.ds(0, SLOT), :]

    def seven(ev):
        return zb_v.at[ev, pl.ds(0, 7), :, pl.ds(0, SLOT + 1), :]

    def piece_start(ev, extra):
        for n in range(2):
            settle(fifteen(xr_v.at[ev, n]), x_r.at[ev, n])
            xr_v[ev, n, chip, 0:SLOT, :] = sb_v[ev, 2 * core + n, chip, 0:SLOT, :]
            acc = xr_v[ev, n, 0, 0:SLOT, :]
            for q in range(1, NQ):
                acc = acc + xr_v[ev, n, q, 0:SLOT, :]
            zb_v[ev, z, n, 0:SLOT, :] = acc
            zb_v[ev, z, n, SLOT : SLOT + 1, :] = jnp.full((1, 128), extra, F32)
        mine = zb_v.at[ev, z, :, pl.ds(0, SLOT + 1), :]
        for k in far_order:
            send(mine, mine, zb_s.at[ev], zb_r.at[ev], zpeer(k))

    def piece_total(ev, n):
        total = zb_v[ev, 0, n, 0 : SLOT + 1, :]
        for k in range(1, NZ):
            total = total + zb_v[ev, k, n, 0 : SLOT + 1, :]
        return total[0:SLOT], total[SLOT : SLOT + 1]

    field_pieces()
    for r in range(ROWS):
        count_copies[r].wait()
        counts = cint_v[r].astype(F32).astype(BF16)
        e_parts = split3(rowv_v[1, r : r + 1, :])
        cx_v[r, 0:128, :] = counts
        cx_v[r, 128:256, :] = expand(e_parts, (128, WIDE))
        for j in range(1, 4):
            ks_v[r, 128 * j : 128 * j + 128, :] = counts
    forward_first()
    backward_all(0)
    prior(0)
    for r in range(ROWS):
        mom = fm_v[:, r, :] + 0.025 * (prior_v[r] + field_lik(r))
        hfield_v[r] = mom
        new = fcur_v[r] + 0.05 * mom
        fcur_v[r] = new
        nf_v[:, r, :] = new
    hs_v[1, 0] = fcur_v[ROWS - 1]
    hs_v[1, 1] = fcur_v[0]
    send(hs_v.at[1, 0], hr_v.at[1, 0], halo_s.at[1, 0], halo_r.at[1, 0], nxt)
    send(hs_v.at[1, 1], hr_v.at[1, 1], halo_s.at[1, 1], halo_r.at[1, 1], prv)
    piece_start(0, jnp.float32(0.0))
    field_pieces()
    energy = prior(1)

    pull = jnp.where(iota((SLOT, 128), 0) < 8, 0.25, 1.0)
    for n in range(2):
        @pl.when(4 * core + 2 * n + chip // 8 != z)
        def _():
            settle(mp_v.at[n, pl.ds(0, SLOT), :], mp_r.at[n])

    settle(seven(0), zb_r.at[0])
    for n in range(2):
        lik, _ = piece_total(0, n)
        q0 = q_v[0, 2 * core + n, chip, 0:SLOT, :]
        half_q = mp_v[n, 0:SLOT, :] + 0.001 * (lik - pull * q0)
        half_v[n, 0:SLOT, :] = half_q
        q_v[1, 2 * core + n, chip, 0:SLOT, :] = q0 + 0.002 * half_q
    mine = q_v.at[1, pl.ds(2 * core, 2), chip, pl.ds(0, SLOT), :]
    for t in turns:
        send(mine, mine, s3_s, s3_r, (2 * chip_at(*t) + core, z))
    settle(q_v.at[1, pl.ds(2 * core, 2), pl.ds(0, NQ - 1), pl.ds(0, SLOT), :], s3_r)
    send(own_set(1), own_set(1), f3_s, f3_r, partner)
    forward_second()
    log_dens = jnp.zeros((1, WIDE), F32)
    for r in range(ROWS):
        log_mix = run_v[0, r : r + 1, :] * LN2 + jnp.log(run_v[1, r : r + 1, :])
        log_joint = run_v[2, r : r + 1, :] * LN2 + jnp.log(run_v[3, r : r + 1, :])
        log_dens = log_dens + rowv_v[0, r : r + 1, :] * (log_joint - log_mix)
    log_part = jnp.sum(log_dens) - energy
    backward_all(1)
    square = jnp.zeros((FAC, WIDE), F32)
    for r in range(ROWS):
        last = hfield_v[r] + 0.025 * (prior_v[r] + field_lik(r))
        nfm_v[:, r, :] = last
        square = square + last * last
    piece_start(1, 0.5 * jnp.sum(square) - log_part)
    nb_v[...] = q_v[1, zc, half, 0:8, :].reshape(64, 128)
    nw_v[...] = unpack_loadings(q_v[1, zc, half, 8, :])
    settle(seven(1), zb_r.at[1])
    weighed = jnp.zeros((SLOT, 128), F32)
    scalar = jnp.zeros((1, 128), F32)
    for n in range(2):
        lik, scalar = piece_total(1, n)
        q1 = q_v[1, 2 * core + n, chip, 0:SLOT, :]
        mom = half_v[n, 0:SLOT, :] + 0.001 * (lik - pull * q1)
        half_v[n, 0:SLOT, :] = mom
        weighed = weighed + 0.5 * (mom * mom) + (0.5 * pull) * (q1 * q1)
    sc_v[c] = scalar + jnp.sum(weighed)
    everyone = [(2 * chip_at(*t) + k, z) for t in turns for k in range(2)] + [partner]
    for peer in everyone:
        send(sc_v.at[c], sc_v.at[c], sc_s, sc_r, peer)

    @pl.when(mom_owner)
    def _():
        mo_v[chip % 8, 0:SLOT, :] = half_v[mom_slot, 0:SLOT, :]
        for peer in everyone:
            send(
                half_v.at[mom_slot, pl.ds(0, SLOT), :], mo_v.at[chip % 8, pl.ds(0, SLOT), :],
                mo_s, mo_r, peer,
            )
        settle(mo_v.at[pl.ds(0, 7), pl.ds(0, SLOT), :], mo_r)

    @pl.when(jnp.logical_not(mom_owner))
    def _():
        settle(mo_v.at[:, pl.ds(0, SLOT), :], mo_r)

    nbm_v[...] = mo_v[:, 0:8, :].reshape(64, 128)
    nwm_v[...] = unpack_loadings(mo_v[:, 8, :])
    settle(sc_v.at[pl.ds(0, NC - 1)], sc_r)
    total = sc_v[0]
    for k in range(1, NC):
        total = total + sc_v[k]
    ham_v[...] = total * (1.0 / 262144.0)

    @pl.when(near)
    def _():
        settle(q_v.at[0, pl.ds(0, 4), pl.ds(0, 14), pl.ds(0, SLOT), :], ag_s)

    def drained(g, carry):
        @pl.when((g // 4 == core) & (g != z))
        def _():
            settle(shard(g), fw_s.at[g])

        return carry

    lax.fori_loop(0, NZ, drained, 0)

    @pl.when(mom_owner)
    def _():
        settle(pm_v.at[pl.ds(0, 7), pl.ds(0, SLOT), :], mp_s)
        settle(tally_v.at[:, pl.ds(0, SLOT), :], mo_s)

    for ev in range(2):
        for n in range(2):
            settle(cb_v.at[ev, n, :, pl.ds(0, SLOT), :], cb_s.at[ev, n])
            settle(fifteen(xr_v.at[ev, n]), x_s.at[ev, n])
            settle(hs_v.at[ev, n], halo_s.at[ev, n])
        settle(seven(ev), zb_s.at[ev])
    settle(q_v.at[1, pl.ds(2 * core, 2), pl.ds(0, NQ - 1), pl.ds(0, SLOT), :], s3_s)
    settle(own_set(1), f3_s)
    settle(ls_v.at[0], land_s.at[0])
    settle(ls_v.at[1], land_s.at[1])
    settle(sc_v.at[pl.ds(0, NC - 1)], sc_s)


def hand_over(*refs):
    sem = refs[-1]
    copies = [pltpu.make_async_copy(refs[i], refs[7 + i], sem.at[i]) for i in range(7)]
    for cp in copies:
        cp.start()
    for cp in copies:
        cp.wait()


def per_device(
    factor_field, profile, mixing, factor_mom, profile_mom, mixing_mom, field_tau,
    counts, land_mask, log_exposure,
):
    hbm = pl.BlockSpec(memory_space=pltpu.MemorySpace.HBM)
    near = pl.BlockSpec(memory_space=pltpu.MemorySpace.VMEM)
    vm = pltpu.VMEM
    dma = pltpu.SemaphoreType.DMA
    shapes = [
        jax.ShapeDtypeStruct(a.shape, F32)
        for a in (factor_field, profile, mixing, factor_mom, profile_mom, mixing_mom)
    ]
    shapes.append(jax.ShapeDtypeStruct((1, 128), F32))
    scratch = [
        vm((FAC, ROWS, WIDE), F32), vm((64, 128), F32), vm((FAC, 64), F32),
        vm((FAC, ROWS, WIDE), F32), vm((64, 128), F32), vm((FAC, 64), F32),
        vm((ROWS, 128, WIDE), jnp.int32), vm((32, WIDE), jnp.int32), vm((32, WIDE), F32),
        vm((2, 4, NQ, 16, 128), F32), vm((8, 16, 128), F32), vm((2, 16, 128), F32),
        vm((2, 16, 128), F32), vm((8, 16, 128), F32), vm((ROWS, 256, WIDE), BF16),
        vm((ROWS, 512, WIDE), BF16), vm((2, 8, WIDE), F32), vm((ROWS, 256, WIDE), BF16),
        vm((384, 128), BF16), vm((512, 128), BF16),
        vm((ROWS, FAC, WIDE), F32), vm((ROWS, FAC, WIDE), F32), vm((ROWS, FAC, WIDE), F32),
        vm((4, ROWS, 128, WIDE), F32), vm((4, ROWS, 128, WIDE), F32),
        vm((4, 8, WIDE), F32), vm((4, 8, WIDE), F32), vm((4, 8, WIDE), F32),
        vm((ROWS, 512, WIDE), BF16), vm((ROWS, 512, WIDE), BF16),
        vm((2, 4, NQ, 16, 128), F32), vm((2, 2, NQ, 16, 128), F32),
        vm((2, 2, NQ, 16, 128), F32), vm((2, NZ, 2, 16, 128), F32),
        vm((2, 2, FAC, WIDE), F32), vm((2, 2, FAC, WIDE), F32),
        vm((2, 1, WIDE), F32), vm((2, 1, WIDE), F32), vm((NC, 1, 128), F32),
        vm((NC - 1, 16, 128), F32),
        dma((8,)), dma((ROWS,)), dma, dma((NZ,)), dma((NZ,)), dma, dma((2,)),
        dma((2, 2)), dma((2, 2)), dma((2, 2)), dma((2, 2)), dma((2,)), dma((2,)),
        dma, dma, dma, dma, dma((2, 2)), dma((2, 2)), dma((2,)), dma((2,)),
        dma, dma, dma, dma,
    ]
    outs = pl.pallas_call(
        leap_kernel,
        out_shape=[vm(s.shape, F32) for s in shapes],
        in_specs=[pl.BlockSpec(memory_space=pltpu.MemorySpace.SMEM)] + [hbm] * 9,
        out_specs=[near] * 7,
        scratch_shapes=scratch,
        compiler_params=pltpu.CompilerParams(
            collective_id=0, has_side_effects=True, vmem_limit_bytes=56 * 1024 * 1024
        ),
        name="leapfrog",
    )(
        field_tau, factor_field, profile, mixing, factor_mom, profile_mom, mixing_mom,
        counts, land_mask, log_exposure,
    )
    outs = pl.pallas_call(
        hand_over,
        out_shape=shapes,
        in_specs=[near] * 7,
        out_specs=[hbm] * 7,
        scratch_shapes=[dma((7,))],
        name="hand_over",
    )(*[pltpu.with_memory_space_constraint(o, pltpu.MemorySpace.VMEM) for o in outs])
    return (*outs[:6], outs[6][0, 0])


def solution(mesh):
    rows = P(None, ("cells", "comp"), None)
    ins = (
        rows, P("comp", None), P(None, "comp"), rows, P("comp", None), P(None, "comp"),
        P(), P(None, "cells", None), P("cells", None), P("cells", None),
    )
    outs = (
        rows, P("comp", None), P(None, "comp"), rows, P("comp", None), P(None, "comp"), P(),
    )
    return jax.shard_map(per_device, mesh=mesh, in_specs=ins, out_specs=outs, check_vma=False)
```

```python
import jax
import jax.numpy as jnp
from jax import lax
from jax.experimental import pallas as pl
from jax.experimental.pallas import tpu as pltpu
from jax.sharding import PartitionSpec as P

F32 = jnp.float32
BF16 = jnp.bfloat16
MESH = pl.DeviceIdType.MESH
NZ = 8
NQ = 16
NC = 32
ROWS = 4
WIDE = 256
FAC = 16
SLOT = 9
LOG2E = 1.4426950408889634
LN2 = 0.6931471805599453


def split3(v):
    hi = v.astype(BF16)
    rest = v - hi.astype(F32)
    mid = rest.astype(BF16)
    low = (rest - mid.astype(F32)).astype(BF16)
    return hi, mid, low


def split2(v):
    hi = v.astype(BF16)
    return hi, (v - hi.astype(F32)).astype(BF16)


def dot(a, b, ca, cb, precision=None):
    return lax.dot_general(
        a, b, (((ca,), (cb,)), ((), ())), precision=precision, preferred_element_type=F32
    )


def iota(shape, dim):
    return lax.broadcasted_iota(jnp.int32, shape, dim)


def own_lanes():
    return (iota((8, 128), 1) // FAC == iota((8, 128), 0))[None]


def packed_rows(wide):
    return jnp.where(own_lanes(), wide.reshape(-1, 8, 128), 0.0).sum(axis=1)


def spread_rows(packed):
    groups = packed.shape[0]
    wide = jnp.broadcast_to(packed[:, None, :], (groups, 8, 128))
    return jnp.where(own_lanes(), wide, 0.0).reshape(groups * 8, 128)


def lane_pick():
    return (iota((FAC, 128), 1) % FAC == iota((FAC, 128), 0)).astype(F32)


def pack_loadings(w):
    return packed_rows(dot(w, lane_pick(), 0, 0, lax.Precision.HIGHEST))


def unpack_loadings(packed):
    return dot(lane_pick(), spread_rows(packed), 1, 1, lax.Precision.HIGHEST)


def leap_kernel(
    tau_ref, f_hbm, b_hbm, w_hbm, fm_hbm, bm_hbm, wm_hbm, c_hbm, land_hbm, loge_hbm,
    nf_v, nb_v, nw_v, nfm_v, mo_o, sc_o,
    f_v, b_v, w_v, fm_v, bm_v, wm_v, cint_v, land_v, loge_v,
    q_v, pm_v, mp_v, half_v, mo_v, cx_v, ks_v, rowv_v, ftile_v, pick_v, w128_v,
    fcur_v, hfield_v, prior_v, ea_v, es_v, gh_v, gl_v,
    sb_v, cb_v, xr_v, zb_v, hs_v, hr_v, ls_v, lr_v, sc_v, tally_v,
    in_sem, cnt_sem, ag_s, ag_r, fw_s, mp_s, mp_r, cb_s, cb_r, x_s, x_r, zb_s, zb_r,
    s3_s, s3_r, f3_s, f3_r, halo_s, halo_r, land_s, land_r, sc_s, sc_r, mo_s, mo_r,
):
    c = lax.axis_index("cells")
    z = lax.axis_index("comp")
    y = c // 8
    x = (c % 8) // 2
    core = c % 2
    chip = c // 2
    place = c * NZ + z
    near = core == z // 4
    zl = (z % 4) // 2 + jnp.where(near, 0, 2)
    far_order = (4, 3, 5, 2, 6, 1, 7)
    partner = (2 * chip + 1 - core, z)

    def zpeer(k):
        return (c, (z + k) % NZ)

    turns = sorted(
        ((a, b) for a in range(4) for b in range(4) if a or b),
        key=lambda t: -(min(t[0], 4 - t[0]) + min(t[1], 4 - t[1])),
    )

    def chip_at(a, b):
        return ((y + a) % 4) * 4 + (x + b) % 4

    after = (place + 1) % 256
    before = (place + 255) % 256
    nxt = (after // NZ, after % NZ)
    prv = (before // NZ, before % NZ)

    def send(src, dst, s_sem, r_sem, peer):
        pltpu.make_async_remote_copy(
            src_ref=src, dst_ref=dst, send_sem=s_sem, recv_sem=r_sem,
            device_id=peer, device_id_type=MESH,
        ).start()

    def settle(ref, sem):
        pltpu.make_async_copy(ref, ref, sem).wait()

    loads = [
        (f_hbm, f_v), (b_hbm, b_v), (w_hbm, w_v), (fm_hbm, fm_v), (bm_hbm, bm_v),
        (wm_hbm, wm_v), (land_hbm, land_v), (loge_hbm, loge_v),
    ]
    copies = [pltpu.make_async_copy(s, d, in_sem.at[i]) for i, (s, d) in enumerate(loads)]
    for cp in copies:
        cp.start()
    count_copies = [
        pltpu.make_async_copy(c_hbm.at[:, ROWS * z + r, :], cint_v.at[r], cnt_sem.at[r])
        for r in range(ROWS)
    ]
    for cp in count_copies:
        cp.start()

    barrier = pltpu.get_barrier_semaphore()
    everyone = [(2 * chip_at(*t) + k, z) for t in turns for k in range(2)] + [partner]
    greeted = everyone[:2] + [zpeer(k) for k in far_order] + [nxt, prv] + everyone[2:]
    for peer in greeted:
        pl.semaphore_signal(barrier, inc=1, device_id=peer, device_id_type=MESH)

    for cp in copies:
        cp.wait()

    half = pl.ds(pl.multiple_of((z % 2) * 8, 8), 8)
    q_v[0, zl, half, 0:8, :] = b_v[...].reshape(8, 8, 128)
    q_v[0, zl, half, 8, :] = pack_loadings(w_v[...])
    pm_v[:, 0:8, :] = bm_v[...].reshape(8, 8, 128)
    pm_v[:, 8, :] = pack_loadings(wm_v[...])
    for r in range(ROWS):
        fcur_v[r] = f_v[:, r, :]
        rowv_v[0, r : r + 1, :] = land_v[pl.ds(ROWS * z + r, 1), :].astype(F32)
        rowv_v[1, r : r + 1, :] = jnp.exp(loge_v[pl.ds(ROWS * z + r, 1), :])
    hs_v[0, 0] = fcur_v[ROWS - 1]
    hs_v[0, 1] = fcur_v[0]
    ls_v[0] = rowv_v[0, ROWS - 1 : ROWS, :]
    ls_v[1] = rowv_v[0, 0:1, :]

    src_lane = iota((384, 128), 0)
    dst_lane = iota((384, 128), 1)
    part = src_lane // 128
    group = dst_lane // FAC
    first = (part == 0) & ((group == 0) | (group == 3) | (group == 5))
    second = (part == 1) & ((group == 1) | (group == 4))
    third = (part == 2) & (group == 2)
    same = src_lane % FAC == dst_lane % FAC
    pick_v[...] = jnp.where(same & (first | second | third), 1.0, 0.0).astype(BF16)

    tau = jnp.zeros((FAC, WIDE), F32)
    fac_row = iota((FAC, WIDE), 0)
    for j in range(FAC):
        tau = jnp.where(fac_row == j, tau_ref[j], tau)

    pl.semaphore_wait(barrier, len(greeted))

    def shard(h):
        return q_v.at[0, h // 2, pl.ds(8 * (h % 2), 8), pl.ds(0, SLOT), :]

    for h in range(4):
        @pl.when(near & (z % 4 == h))
        def _():
            for k in far_order:
                send(shard(h), shard(h), ag_s, ag_r.at[h], zpeer(k))

    send(hs_v.at[0, 0], hr_v.at[0, 0], halo_s.at[0, 0], halo_r.at[0, 0], nxt)
    send(hs_v.at[0, 1], hr_v.at[0, 1], halo_s.at[0, 1], halo_r.at[0, 1], prv)
    send(ls_v.at[0], lr_v.at[0], land_s.at[0], land_r.at[0], nxt)
    send(ls_v.at[1], lr_v.at[1], land_s.at[1], land_r.at[1], prv)
    mom_owner = near & (z % 2 == chip // 8)
    mom_slot = (z % 4) // 2

    @pl.when(mom_owner)
    def _():
        mp_v[mom_slot, 0:SLOT, :] = pm_v[chip % 8, 0:SLOT, :]
        for k in far_order:
            send(
                pm_v.at[chip % 8, pl.ds(0, SLOT), :], mp_v.at[mom_slot, pl.ds(0, SLOT), :],
                mp_s, mp_r.at[mom_slot], zpeer(k),
            )

    def expand(parts, shape):
        row = iota(shape, 0)
        out = jnp.zeros(shape, F32)
        for i, v in enumerate(parts):
            out = jnp.where(row == i, v.astype(F32), out)
        return out.astype(BF16)

    def field_pieces():
        for r in range(ROWS):
            hi, mid, low = split3(fcur_v[r])
            e_hi, e_mid, e_low = split3(rowv_v[1, r : r + 1, :])
            shares = expand((e_hi, e_mid, e_low, e_hi, e_mid, e_hi), (FAC, WIDE))
            none = jnp.zeros((FAC, WIDE), BF16)
            ks_v[r, 0:128, :] = jnp.concatenate(
                [hi, hi, hi, mid, mid, low, shares, none], axis=0
            )
            ftile_v[r] = jnp.concatenate([hi] * 8 + [mid] * 8, axis=0)

    def prior(ev):
        settle(hr_v.at[ev, 0], halo_r.at[ev, 0])
        settle(hr_v.at[ev, 1], halo_r.at[ev, 1])
        if ev == 0:
            settle(lr_v.at[0], land_r.at[0])
            settle(lr_v.at[1], land_r.at[1])
        land_prev = jnp.where(place > 0, lr_v[0], 0.0)
        land_next = jnp.where(place < 255, lr_v[1], 0.0)
        fields = [hr_v[ev, 0]] + [fcur_v[r] for r in range(ROWS)] + [hr_v[ev, 1]]
        lands = [land_prev] + [rowv_v[0, r : r + 1, :] for r in range(ROWS)] + [land_next]
        steps = [fields[i + 1] - fields[i] for i in range(ROWS + 1)]
        flux = [(lands[i + 1] * lands[i]) * steps[i] for i in range(ROWS + 1)]
        energy = jnp.zeros((FAC, WIDE), F32)
        lane = iota((1, WIDE), 1)
        for r in range(ROWS):
            centre, land = fields[r + 1], lands[r + 1]
            step_y = pltpu.roll(centre, WIDE - 1, 1) - centre
            edge_y = jnp.where(lane < WIDE - 1, pltpu.roll(land, WIDE - 1, 1) * land, 0.0)
            flux_y = edge_y * step_y
            back = jnp.where(lane > 0, pltpu.roll(flux_y, 1, 1), 0.0)
            lap = (flux[r] - flux[r + 1]) + (back - flux_y)
            prior_v[r] = -tau * (lap + 0.1 * centre)
            energy = energy + (
                flux[r + 1] * steps[r + 1] + flux_y * step_y + 0.1 * (centre * centre)
            )
        return 0.5 * jnp.sum(tau * energy)

    def profiles(ev, part):
        return q_v[ev, 2 * part : 2 * part + 2, :, 0:8, :].reshape(256, 128)

    def forward(ev, part):
        b = profiles(ev, part)
        wide = spread_rows(q_v[ev, 2 * part : 2 * part + 2, :, 8, :].reshape(32, 128))
        spread = dot(jnp.concatenate(split3(wide * LOG2E), axis=1), pick_v[...], 1, 0)
        rate = jnp.sum(jnp.exp(b), axis=1, keepdims=True) * (-LOG2E)
        r_hi, r_mid, r_low = [v.astype(F32) for v in split3(rate)]
        lane = iota((256, 128), 1)
        shares = jnp.where(
            lane < 96, spread,
            jnp.where(lane < 99, r_hi, jnp.where(lane < 101, r_mid, jnp.where(lane < 102, r_low, 0.0))),
        )
        w128 = spread.astype(BF16)
        w128_v[256 * part : 256 * part + 256, :] = w128
        lhs = jnp.concatenate([shares.astype(BF16)] + list(split3(b * LOG2E)), axis=1)
        stats = []
        for r in range(ROWS):
            a = dot(w128, ks_v[r, 0:128, :], 1, 0)
            s = dot(lhs, ks_v[r], 1, 0)
            for v, e_ref in ((a, ea_v), (s, es_v)):
                top = jnp.max(v, axis=0, keepdims=True)
                e = jnp.exp2(v - top)
                e_ref[part, r] = e
                stats.append((top, jnp.sum(e, axis=0, keepdims=True)))
        return stats

    def joined(one, two):
        out = []
        for (top_0, sum_0), (top_1, sum_1) in zip(one, two):
            top = jnp.maximum(top_0, top_1)
            up_0, up_1 = jnp.exp2(top_0 - top), jnp.exp2(top_1 - top)
            out.append((top, sum_0 * up_0 + sum_1 * up_1, up_0, up_1))
        return out

    def scales(total):
        out = [[], []]
        for k, (_, mass, up_0, up_1) in enumerate(total):
            inv = rowv_v[0, k // 2 : k // 2 + 1, :] / mass
            out[0].append(up_0 * inv)
            out[1].append(up_1 * inv)
        return out

    def own_set(ev):
        return q_v.at[ev, 0:2, :, pl.ds(0, SLOT), :]

    def other_set(ev):
        return q_v.at[ev, 2:4, :, pl.ds(0, SLOT), :]

    def forward_first():
        for h in range(4):
            @pl.when(jnp.logical_not(near & (z % 4 == h)))
            def _():
                settle(shard(h), ag_r.at[h])
                send(shard(h), shard(4 + h), fw_s.at[h], ag_r.at[4 + h], partner)

        one = forward(0, 0)
        for h in range(4):
            @pl.when(near | (z % 4 != h))
            def _():
                settle(shard(4 + h), ag_r.at[4 + h])

        return joined(one, forward(0, 1))

    def forward_second():
        one = forward(1, 0)
        settle(other_set(1), f3_r)
        return joined(one, forward(1, 1))

    def backward(ev, part, scale):
        b = profiles(ev, part)
        gc = jnp.zeros((512, 256), F32)
        gw = jnp.zeros((512, 256), F32)
        for r in range(ROWS):
            p = es_v[part, r] * scale[2 * r + 1]
            gap = p - ea_v[part, r] * scale[2 * r]
            gc = gc + dot(jnp.concatenate(split2(p), axis=0), cx_v[r], 1, 1)
            hi, low = split2(gap)
            gw = gw + dot(jnp.concatenate([hi, low], axis=0), ftile_v[r], 1, 1)
            gh_v[r, 256 * part : 256 * part + 256, :] = hi
            gl_v[r, 256 * part : 256 * part + 256, :] = low
        both = gc[0:256] + gc[256:512]
        rate_mass = jnp.sum(both[:, 128:256], axis=1, keepdims=True)
        gb = both[:, 0:128] - jnp.exp(b) * rate_mass
        wide = (gw[256:512, 128:256] + gw[256:512, 0:128]) + gw[0:256, 128:256]
        return (
            gb.reshape(2, 16, 8, 128),
            packed_rows(wide + gw[0:256, 0:128]).reshape(2, 16, 128),
        )

    def backward_all(ev, total):
        scale = scales(total)
        gb, gw = backward(ev, 1, scale[1])
        sb_v[ev, 2:4, :, 0:8, :] = gb
        sb_v[ev, 2:4, :, 8, :] = gw
        send(
            sb_v.at[ev, 2:4, :, pl.ds(0, SLOT), :], cb_v.at[ev, :, :, pl.ds(0, SLOT), :],
            cb_s.at[ev], cb_r.at[ev], partner,
        )
        gb, gw = backward(ev, 0, scale[0])
        settle(cb_v.at[ev, :, :, pl.ds(0, SLOT), :], cb_r.at[ev])
        sb_v[ev, 0:2, :, 0:8, :] = gb + cb_v[ev, :, :, 0:8, :]
        sb_v[ev, 0:2, :, 8, :] = gw + cb_v[ev, :, :, 8, :]
        for t in turns:
            to = chip_at(*t)
            send(
                sb_v.at[ev, 0:2, to, pl.ds(0, SLOT), :],
                xr_v.at[ev, :, chip, pl.ds(0, SLOT), :],
                x_s.at[ev], x_r.at[ev], (2 * to + core, z),
            )

    def field_lik(r):
        both = dot(w128_v[...], gh_v[r], 0, 0) + dot(w128_v[...], gl_v[r], 0, 0)
        return ((both[32:48] + both[16:32]) + both[0:16]) * LN2

    def fifteen(ev):
        return xr_v.at[ev, :, pl.ds(0, NQ - 1), pl.ds(0, SLOT), :]

    def seven(ev):
        return zb_v.at[ev, pl.ds(0, 7), :, pl.ds(0, SLOT + 1), :]

    def piece_start(ev, extra):
        settle(fifteen(ev), x_r.at[ev])
        for n in range(2):
            xr_v[ev, n, chip, 0:SLOT, :] = sb_v[ev, n, chip, 0:SLOT, :]
            acc = xr_v[ev, n, 0, 0:SLOT, :]
            for q in range(1, NQ):
                acc = acc + xr_v[ev, n, q, 0:SLOT, :]
            zb_v[ev, z, n, 0:SLOT, :] = acc
            zb_v[ev, z, n, SLOT : SLOT + 1, :] = jnp.full((1, 128), extra, F32)
        mine = zb_v.at[ev, z, :, pl.ds(0, SLOT + 1), :]
        for k in far_order:
            send(mine, mine, zb_s.at[ev], zb_r.at[ev], zpeer(k))

    def piece_total(ev, n):
        total = zb_v[ev, 0, n, 0 : SLOT + 1, :]
        for k in range(1, NZ):
            total = total + zb_v[ev, k, n, 0 : SLOT + 1, :]
        return total[0:SLOT], total[SLOT : SLOT + 1]

    field_pieces()
    for r in range(ROWS):
        count_copies[r].wait()
        counts = cint_v[r].astype(F32).astype(BF16)
        e_parts = split3(rowv_v[1, r : r + 1, :])
        cx_v[r, 0:128, :] = counts
        cx_v[r, 128:256, :] = expand(e_parts, (128, WIDE))
        for j in range(1, 4):
            ks_v[r, 128 * j : 128 * j + 128, :] = counts
    backward_all(0, forward_first())
    prior(0)
    for r in range(ROWS):
        mom = fm_v[:, r, :] + 0.025 * (prior_v[r] + field_lik(r))
        hfield_v[r] = mom
        new = fcur_v[r] + 0.05 * mom
        fcur_v[r] = new
        nf_v[:, r, :] = new
    hs_v[1, 0] = fcur_v[ROWS - 1]
    hs_v[1, 1] = fcur_v[0]
    send(hs_v.at[1, 0], hr_v.at[1, 0], halo_s.at[1, 0], halo_r.at[1, 0], nxt)
    send(hs_v.at[1, 1], hr_v.at[1, 1], halo_s.at[1, 1], halo_r.at[1, 1], prv)
    piece_start(0, jnp.float32(0.0))
    field_pieces()
    energy = prior(1)

    pull = jnp.where(iota((SLOT, 128), 0) < 8, 0.25, 1.0)
    for n in range(2):
        @pl.when(4 * core + 2 * n + chip // 8 != z)
        def _():
            settle(mp_v.at[n, pl.ds(0, SLOT), :], mp_r.at[n])

    settle(seven(0), zb_r.at[0])
    for n in range(2):
        lik, _ = piece_total(0, n)
        q0 = q_v[0, n, chip, 0:SLOT, :]
        half_q = mp_v[n, 0:SLOT, :] + 0.001 * (lik - pull * q0)
        half_v[n, 0:SLOT, :] = half_q
        q_v[1, n, chip, 0:SLOT, :] = q0 + 0.002 * half_q
    mine = q_v.at[1, 0:2, chip, pl.ds(0, SLOT), :]
    for t in turns:
        send(mine, mine, s3_s, s3_r, (2 * chip_at(*t) + core, z))
    settle(q_v.at[1, 0:2, pl.ds(0, NQ - 1), pl.ds(0, SLOT), :], s3_r)
    send(own_set(1), other_set(1), f3_s, f3_r, partner)
    total = forward_second()
    backward_all(1, total)
    log_dens = jnp.zeros((1, WIDE), F32)
    for r in range(ROWS):
        log_mix = total[2 * r][0] * LN2 + jnp.log(total[2 * r][1])
        log_joint = total[2 * r + 1][0] * LN2 + jnp.log(total[2 * r + 1][1])
        log_dens = log_dens + rowv_v[0, r : r + 1, :] * (log_joint - log_mix)
    log_part = jnp.sum(log_dens) - energy
    square = jnp.zeros((FAC, WIDE), F32)
    for r in range(ROWS):
        last = hfield_v[r] + 0.025 * (prior_v[r] + field_lik(r))
        nfm_v[:, r, :] = last
        square = square + last * last
    piece_start(1, 0.5 * jnp.sum(square) - log_part)

    @pl.when(near)
    def _():
        settle(q_v.at[0, pl.ds(0, 4), pl.ds(0, 14), pl.ds(0, SLOT), :], ag_s)

    @pl.when(mom_owner)
    def _():
        settle(pm_v.at[pl.ds(0, 7), pl.ds(0, SLOT), :], mp_s)

    for h in range(4):
        @pl.when(jnp.logical_not(near & (z % 4 == h)))
        def _():
            settle(shard(h), fw_s.at[h])

    for ev in range(2):
        settle(cb_v.at[ev, :, :, pl.ds(0, SLOT), :], cb_s.at[ev])
        settle(fifteen(ev), x_s.at[ev])
        settle(seven(ev), zb_s.at[ev])
        for n in range(2):
            settle(hs_v.at[ev, n], halo_s.at[ev, n])
    settle(q_v.at[1, 0:2, pl.ds(0, NQ - 1), pl.ds(0, SLOT), :], s3_s)
    settle(own_set(1), f3_s)
    settle(ls_v.at[0], land_s.at[0])
    settle(ls_v.at[1], land_s.at[1])
    nb_v[...] = q_v[1, zl, half, 0:8, :].reshape(64, 128)
    nw_v[...] = unpack_loadings(q_v[1, zl, half, 8, :])
    settle(seven(1), zb_r.at[1])
    weighed = jnp.zeros((SLOT, 128), F32)
    scalar = jnp.zeros((1, 128), F32)
    for n in range(2):
        lik, scalar = piece_total(1, n)
        q1 = q_v[1, n, chip, 0:SLOT, :]
        mom = half_v[n, 0:SLOT, :] + 0.001 * (lik - pull * q1)
        half_v[n, 0:SLOT, :] = mom
        weighed = weighed + 0.5 * (mom * mom) + (0.5 * pull) * (q1 * q1)
    sc_v[c] = scalar + jnp.sum(weighed)

    @pl.when(mom_owner)
    def _():
        mo_v[chip % 8, 0:SLOT, :] = half_v[mom_slot, 0:SLOT, :]
        for peer in everyone:
            send(sc_v.at[c], sc_v.at[c], sc_s, sc_r, peer)
            send(
                half_v.at[mom_slot, pl.ds(0, SLOT), :], mo_v.at[chip % 8, pl.ds(0, SLOT), :],
                mo_s, mo_r, peer,
            )
        settle(mo_v.at[pl.ds(0, 7), pl.ds(0, SLOT), :], mo_r)

    @pl.when(jnp.logical_not(mom_owner))
    def _():
        for peer in everyone:
            send(sc_v.at[c], sc_v.at[c], sc_s, sc_r, peer)
        settle(mo_v.at[:, pl.ds(0, SLOT), :], mo_r)

    mo_o[:, 0:SLOT, :] = mo_v[:, 0:SLOT, :]
    settle(sc_v.at[pl.ds(0, NC - 1)], sc_r)
    sc_o[...] = sc_v[...]

    settle(sc_v.at[pl.ds(0, NC - 1)], sc_s)

    @pl.when(mom_owner)
    def _():
        settle(tally_v.at[:, pl.ds(0, SLOT), :], mo_s)


def hand_over(
    nf_v, nb_v, nw_v, nfm_v, mo_v, sc_v,
    nf_hbm, nb_hbm, nw_hbm, nfm_hbm, nbm_hbm, nwm_hbm, ham_hbm, nbm_v, nwm_v, ham_v, sem,
):
    moves = (
        (nf_v, nf_hbm), (nb_v, nb_hbm), (nw_v, nw_hbm), (nfm_v, nfm_hbm),
        (nbm_v, nbm_hbm), (nwm_v, nwm_hbm), (ham_v, ham_hbm),
    )
    copies = [pltpu.make_async_copy(s, d, sem.at[i]) for i, (s, d) in enumerate(moves)]
    for cp in copies[:4]:
        cp.start()
    nbm_v[...] = mo_v[:, 0:8, :].reshape(64, 128)
    nwm_v[...] = unpack_loadings(mo_v[:, 8, :])
    total = sc_v[0]
    for k in range(1, NC):
        total = total + sc_v[k]
    ham_v[...] = total * (1.0 / 262144.0)
    for cp in copies[4:]:
        cp.start()
    for cp in copies:
        cp.wait()


def per_device(
    factor_field, profile, mixing, factor_mom, profile_mom, mixing_mom, field_tau,
    counts, land_mask, log_exposure,
):
    hbm = pl.BlockSpec(memory_space=pltpu.MemorySpace.HBM)
    near = pl.BlockSpec(memory_space=pltpu.MemorySpace.VMEM)
    vm = pltpu.VMEM
    dma = pltpu.SemaphoreType.DMA
    shapes = [
        jax.ShapeDtypeStruct(a.shape, F32)
        for a in (factor_field, profile, mixing, factor_mom, profile_mom, mixing_mom)
    ]
    shapes.append(jax.ShapeDtypeStruct((1, 128), F32))
    scratch = [
        vm((FAC, ROWS, WIDE), F32), vm((64, 128), F32), vm((FAC, 64), F32),
        vm((FAC, ROWS, WIDE), F32), vm((64, 128), F32), vm((FAC, 64), F32),
        vm((ROWS, 128, WIDE), jnp.int32), vm((32, WIDE), jnp.int32), vm((32, WIDE), F32),
        vm((2, 4, NQ, 16, 128), F32), vm((8, 16, 128), F32), vm((2, 16, 128), F32),
        vm((2, 16, 128), F32), vm((8, 16, 128), F32), vm((ROWS, 256, WIDE), BF16),
        vm((ROWS, 512, WIDE), BF16), vm((2, 8, WIDE), F32), vm((ROWS, 256, WIDE), BF16),
        vm((384, 128), BF16), vm((512, 128), BF16),
        vm((ROWS, FAC, WIDE), F32), vm((ROWS, FAC, WIDE), F32), vm((ROWS, FAC, WIDE), F32),
        vm((2, ROWS, 256, WIDE), F32), vm((2, ROWS, 256, WIDE), F32),
        vm((ROWS, 512, WIDE), BF16), vm((ROWS, 512, WIDE), BF16),
        vm((2, 4, NQ, 16, 128), F32), vm((2, 2, NQ, 16, 128), F32),
        vm((2, 2, NQ, 16, 128), F32), vm((2, NZ, 2, 16, 128), F32),
        vm((2, 2, FAC, WIDE), F32), vm((2, 2, FAC, WIDE), F32),
        vm((2, 1, WIDE), F32), vm((2, 1, WIDE), F32), vm((NC, 1, 128), F32),
        vm((NC - 1, 16, 128), F32),
        dma((8,)), dma((ROWS,)), dma, dma((NZ,)), dma((NZ,)), dma, dma((2,)),
        dma((2,)), dma((2,)), dma((2,)), dma((2,)), dma((2,)), dma((2,)),
        dma, dma, dma, dma, dma((2, 2)), dma((2, 2)), dma((2,)), dma((2,)),
        dma, dma, dma, dma,
    ]
    outs = pl.pallas_call(
        leap_kernel,
        out_shape=[vm(s.shape, F32) for s in shapes[:4]]
        + [vm((8, 16, 128), F32), vm((NC, 1, 128), F32)],
        in_specs=[pl.BlockSpec(memory_space=pltpu.MemorySpace.SMEM)] + [hbm] * 9,
        out_specs=[near] * 6,
        scratch_shapes=scratch,
        compiler_params=pltpu.CompilerParams(
            collective_id=0, has_side_effects=True, vmem_limit_bytes=56 * 1024 * 1024
        ),
        name="leapfrog",
    )(
        field_tau, factor_field, profile, mixing, factor_mom, profile_mom, mixing_mom,
        counts, land_mask, log_exposure,
    )
    outs = pl.pallas_call(
        hand_over,
        out_shape=shapes,
        in_specs=[near] * 6,
        out_specs=[hbm] * 7,
        scratch_shapes=[vm((64, 128), F32), vm((FAC, 64), F32), vm((1, 128), F32), dma((7,))],
        name="hand_over",
    )(*[pltpu.with_memory_space_constraint(o, pltpu.MemorySpace.VMEM) for o in outs])
    return (*outs[:6], outs[6][0, 0])


def solution(mesh):
    rows = P(None, ("cells", "comp"), None)
    ins = (
        rows, P("comp", None), P(None, "comp"), rows, P("comp", None), P(None, "comp"),
        P(), P(None, "cells", None), P("cells", None), P("cells", None),
    )
    outs = (
        rows, P("comp", None), P(None, "comp"), rows, P("comp", None), P(None, "comp"), P(),
    )
    return jax.shard_map(per_device, mesh=mesh, in_specs=ins, out_specs=outs, check_vma=False)
```

```python
import jax
import jax.numpy as jnp
from jax import lax
from jax.experimental import pallas as pl
from jax.experimental.pallas import tpu as pltpu
from jax.sharding import PartitionSpec as P

F32 = jnp.float32
BF16 = jnp.bfloat16
MESH = pl.DeviceIdType.MESH
NZ = 8
NQ = 16
NC = 32
ROWS = 4
WIDE = 256
FAC = 16
SLOT = 9
LOG2E = 1.4426950408889634
LN2 = 0.6931471805599453


def split3(v):
    hi = v.astype(BF16)
    rest = v - hi.astype(F32)
    mid = rest.astype(BF16)
    low = (rest - mid.astype(F32)).astype(BF16)
    return hi, mid, low


def split2(v):
    hi = v.astype(BF16)
    return hi, (v - hi.astype(F32)).astype(BF16)


def dot(a, b, ca, cb, precision=None):
    return lax.dot_general(
        a, b, (((ca,), (cb,)), ((), ())), precision=precision, preferred_element_type=F32
    )


def iota(shape, dim):
    return lax.broadcasted_iota(jnp.int32, shape, dim)


def own_lanes():
    return (iota((8, 128), 1) // FAC == iota((8, 128), 0))[None]


def packed_rows(wide):
    return jnp.where(own_lanes(), wide.reshape(-1, 8, 128), 0.0).sum(axis=1)


def spread_rows(packed):
    groups = packed.shape[0]
    wide = jnp.broadcast_to(packed[:, None, :], (groups, 8, 128))
    return jnp.where(own_lanes(), wide, 0.0).reshape(groups * 8, 128)


def lane_pick():
    return (iota((FAC, 128), 1) % FAC == iota((FAC, 128), 0)).astype(F32)


def pack_loadings(w):
    return packed_rows(dot(w, lane_pick(), 0, 0, lax.Precision.HIGHEST))


def unpack_loadings(packed):
    return dot(lane_pick(), spread_rows(packed), 1, 1, lax.Precision.HIGHEST)


def leap_kernel(
    tau_hbm, f_hbm, b_hbm, w_hbm, fm_hbm, bm_hbm, wm_hbm, c_hbm, land_hbm, loge_hbm,
    nf_v, nb_v, nw_v, nfm_v, mo_o, sc_o,
    f_v, b_v, w_v, fm_v, bm_v, wm_v, cint_v, land_v, loge_v,
    q_v, pm_v, mp_v, half_v, mo_v, cx_v, ks_v, rowv_v, ftile_v, pick_v, w128_v,
    fcur_v, hfield_v, prior_v, ea_v, es_v, gh_v, gl_v,
    sb_v, cb_v, xr_v, zb_v, hs_v, hr_v, ls_v, lr_v, sc_v, tally_v, tau_ref,
    in_sem, cnt_sem, ag_s, ag_r, fw_s, fw_r, mp_s, mp_r, cb_s, cb_r, x_s, x_r, zb_s, zb_r,
    s3_s, s3_r, f3_s, f3_r, halo_s, halo_r, land_s, land_r, sc_s, sc_r, mo_s, mo_r,
):
    c = lax.axis_index("cells")
    z = lax.axis_index("comp")
    y = c // 8
    x = (c % 8) // 2
    core = c % 2
    chip = c // 2
    place = c * NZ + z
    far_order = (4, 3, 5, 2, 6, 1, 7)
    partner = (2 * chip + 1 - core, z)

    def zpeer(k):
        return (c, (z + k) % NZ)

    turns = sorted(
        ((a, b) for a in range(4) for b in range(4) if a or b),
        key=lambda t: -(min(t[0], 4 - t[0]) + min(t[1], 4 - t[1])),
    )

    def chip_at(a, b):
        return ((y + a) % 4) * 4 + (x + b) % 4

    after = (place + 1) % 256
    before = (place + 255) % 256
    nxt = (after // NZ, after % NZ)
    prv = (before // NZ, before % NZ)

    def send(src, dst, s_sem, r_sem, peer):
        pltpu.make_async_remote_copy(
            src_ref=src, dst_ref=dst, send_sem=s_sem, recv_sem=r_sem,
            device_id=peer, device_id_type=MESH,
        ).start()

    def settle(ref, sem):
        pltpu.make_async_copy(ref, ref, sem).wait()

    barrier = pltpu.get_barrier_semaphore()
    everyone = [(2 * chip_at(*t) + k, z) for t in turns for k in range(2)] + [partner]
    greeted = everyone[:2] + [zpeer(k) for k in far_order] + [nxt, prv] + everyone[2:]
    for peer in greeted:
        pl.semaphore_signal(barrier, inc=1, device_id=peer, device_id_type=MESH)

    loads = [
        (f_hbm, f_v), (b_hbm, b_v), (w_hbm, w_v), (fm_hbm, fm_v), (bm_hbm, bm_v),
        (wm_hbm, wm_v), (land_hbm, land_v), (loge_hbm, loge_v), (tau_hbm, tau_ref),
    ]
    copies = [pltpu.make_async_copy(s, d, in_sem.at[i]) for i, (s, d) in enumerate(loads)]
    for cp in copies:
        cp.start()
    count_copies = [
        pltpu.make_async_copy(c_hbm.at[:, ROWS * z + r, :], cint_v.at[r], cnt_sem.at[r])
        for r in range(ROWS)
    ]
    for cp in count_copies:
        cp.start()

    for cp in copies:
        cp.wait()

    side = z // 4
    span = pl.ds(4 * (z % 4), 4)
    blocks = b_v[...].reshape(8, 8, 128)
    strips = pack_loadings(w_v[...])
    q_v[0, side, span, 0:8, :] = jnp.where(core == 0, blocks[0:4], blocks[4:8])
    q_v[0, side, span, 8, :] = jnp.where(core == 0, strips[0:4], strips[4:8])
    q_v[0, 2 + side, span, 0:8, :] = jnp.where(core == 0, blocks[4:8], blocks[0:4])
    q_v[0, 2 + side, span, 8, :] = jnp.where(core == 0, strips[4:8], strips[0:4])
    pm_v[:, 0:8, :] = bm_v[...].reshape(8, 8, 128)
    pm_v[:, 8, :] = pack_loadings(wm_v[...])
    for r in range(ROWS):
        fcur_v[r] = f_v[:, r, :]
        rowv_v[0, r : r + 1, :] = land_v[pl.ds(ROWS * z + r, 1), :].astype(F32)
        rowv_v[1, r : r + 1, :] = jnp.exp(loge_v[pl.ds(ROWS * z + r, 1), :])
    hs_v[0, 0] = fcur_v[ROWS - 1]
    hs_v[0, 1] = fcur_v[0]
    ls_v[0] = rowv_v[0, ROWS - 1 : ROWS, :]
    ls_v[1] = rowv_v[0, 0:1, :]

    src_lane = iota((384, 128), 0)
    dst_lane = iota((384, 128), 1)
    part = src_lane // 128
    group = dst_lane // FAC
    first = (part == 0) & ((group == 0) | (group == 3) | (group == 5))
    second = (part == 1) & ((group == 1) | (group == 4))
    third = (part == 2) & (group == 2)
    same = src_lane % FAC == dst_lane % FAC
    pick_v[...] = jnp.where(same & (first | second | third), 1.0, 0.0).astype(BF16)

    tau = jnp.zeros((FAC, WIDE), F32)
    fac_row = iota((FAC, WIDE), 0)
    for j in range(FAC):
        tau = jnp.where(fac_row == j, tau_ref[j], tau)

    pl.semaphore_wait(barrier, len(greeted))

    def shard(g, base):
        return q_v.at[0, base + g // 4, pl.ds(4 * (g % 4), 4), pl.ds(0, SLOT), :]

    for k in far_order:
        send(shard(z, 0), shard(z, 0), ag_s, ag_r.at[z], zpeer(k))

    mom_owner = z % 4 == chip // 4
    mom_piece = 4 * core + chip % 4

    def send_extras():
        send(hs_v.at[0, 0], hr_v.at[0, 0], halo_s.at[0, 0], halo_r.at[0, 0], nxt)
        send(hs_v.at[0, 1], hr_v.at[0, 1], halo_s.at[0, 1], halo_r.at[0, 1], prv)
        send(ls_v.at[0], lr_v.at[0], land_s.at[0], land_r.at[0], nxt)
        send(ls_v.at[1], lr_v.at[1], land_s.at[1], land_r.at[1], prv)

        @pl.when(mom_owner)
        def _():
            mp_v[side, 0:SLOT, :] = pm_v[mom_piece, 0:SLOT, :]
            for k in far_order:
                send(
                    pm_v.at[mom_piece, pl.ds(0, SLOT), :], mp_v.at[side, pl.ds(0, SLOT), :],
                    mp_s, mp_r.at[side], zpeer(k),
                )

    def expand(parts, shape):
        row = iota(shape, 0)
        out = jnp.zeros(shape, F32)
        for i, v in enumerate(parts):
            out = jnp.where(row == i, v.astype(F32), out)
        return out.astype(BF16)

    def field_pieces():
        for r in range(ROWS):
            hi, mid, low = split3(fcur_v[r])
            e_hi, e_mid, e_low = split3(rowv_v[1, r : r + 1, :])
            shares = expand((e_hi, e_mid, e_low, e_hi, e_mid, e_hi), (FAC, WIDE))
            none = jnp.zeros((FAC, WIDE), BF16)
            ks_v[r, 0:128, :] = jnp.concatenate(
                [hi, hi, hi, mid, mid, low, shares, none], axis=0
            )
            ftile_v[r] = jnp.concatenate([hi] * 8 + [mid] * 8, axis=0)

    def prior(ev):
        settle(hr_v.at[ev, 0], halo_r.at[ev, 0])
        settle(hr_v.at[ev, 1], halo_r.at[ev, 1])
        if ev == 0:
            settle(lr_v.at[0], land_r.at[0])
            settle(lr_v.at[1], land_r.at[1])
        land_prev = jnp.where(place > 0, lr_v[0], 0.0)
        land_next = jnp.where(place < 255, lr_v[1], 0.0)
        fields = [hr_v[ev, 0]] + [fcur_v[r] for r in range(ROWS)] + [hr_v[ev, 1]]
        lands = [land_prev] + [rowv_v[0, r : r + 1, :] for r in range(ROWS)] + [land_next]
        steps = [fields[i + 1] - fields[i] for i in range(ROWS + 1)]
        flux = [(lands[i + 1] * lands[i]) * steps[i] for i in range(ROWS + 1)]
        energy = jnp.zeros((FAC, WIDE), F32)
        lane = iota((1, WIDE), 1)
        for r in range(ROWS):
            centre, land = fields[r + 1], lands[r + 1]
            step_y = pltpu.roll(centre, WIDE - 1, 1) - centre
            edge_y = jnp.where(lane < WIDE - 1, pltpu.roll(land, WIDE - 1, 1) * land, 0.0)
            flux_y = edge_y * step_y
            back = jnp.where(lane > 0, pltpu.roll(flux_y, 1, 1), 0.0)
            lap = (flux[r] - flux[r + 1]) + (back - flux_y)
            prior_v[r] = -tau * (lap + 0.1 * centre)
            energy = energy + (
                flux[r + 1] * steps[r + 1] + flux_y * step_y + 0.1 * (centre * centre)
            )
        return 0.5 * jnp.sum(tau * energy)

    def profiles(ev, part):
        return q_v[ev, 2 * part : 2 * part + 2, :, 0:8, :].reshape(256, 128)

    def forward(ev, part):
        b = profiles(ev, part)
        wide = spread_rows(q_v[ev, 2 * part : 2 * part + 2, :, 8, :].reshape(32, 128))
        spread = dot(jnp.concatenate(split3(wide * LOG2E), axis=1), pick_v[...], 1, 0)
        rate = jnp.sum(jnp.exp(b), axis=1, keepdims=True) * (-LOG2E)
        r_hi, r_mid, r_low = [v.astype(F32) for v in split3(rate)]
        lane = iota((256, 128), 1)
        shares = jnp.where(
            lane < 96, spread,
            jnp.where(lane < 99, r_hi, jnp.where(lane < 101, r_mid, jnp.where(lane < 102, r_low, 0.0))),
        )
        w128 = spread.astype(BF16)
        w128_v[256 * part : 256 * part + 256, :] = w128
        lhs = jnp.concatenate([shares.astype(BF16)] + list(split3(b * LOG2E)), axis=1)
        stats = []
        for r in range(ROWS):
            a = dot(w128, ks_v[r, 0:128, :], 1, 0)
            s = dot(lhs, ks_v[r], 1, 0)
            for v, e_ref in ((a, ea_v), (s, es_v)):
                top = jnp.max(v, axis=0, keepdims=True)
                e = jnp.exp2(v - top)
                e_ref[part, r] = e
                stats.append((top, jnp.sum(e, axis=0, keepdims=True)))
        return stats

    def joined(one, two):
        out = []
        for (top_0, sum_0), (top_1, sum_1) in zip(one, two):
            top = jnp.maximum(top_0, top_1)
            up_0, up_1 = jnp.exp2(top_0 - top), jnp.exp2(top_1 - top)
            out.append((top, sum_0 * up_0 + sum_1 * up_1, up_0, up_1))
        return out

    def scales(total):
        out = [[], []]
        for k, (_, mass, up_0, up_1) in enumerate(total):
            inv = rowv_v[0, k // 2 : k // 2 + 1, :] / mass
            out[0].append(up_0 * inv)
            out[1].append(up_1 * inv)
        return out

    def own_set(ev):
        return q_v.at[ev, 0:2, :, pl.ds(0, SLOT), :]

    def other_set(ev):
        return q_v.at[ev, 2:4, :, pl.ds(0, SLOT), :]

    def seven_shards(base):
        return q_v.at[0, base : base + 2, pl.ds(0, 14), pl.ds(0, SLOT), :]

    def forward_first():
        for k in far_order:
            g = (z + k) % NZ
            settle(shard(g, 0), ag_r.at[g])
            send(shard(g, 0), shard(g, 2), fw_s, fw_r, partner)
        send_extras()
        one = forward(0, 0)
        settle(seven_shards(2), fw_r)
        return joined(one, forward(0, 1))

    def forward_second():
        one = forward(1, 0)
        settle(other_set(1), f3_r)
        return joined(one, forward(1, 1))

    def backward(ev, part, scale):
        b = profiles(ev, part)
        gc = jnp.zeros((512, 256), F32)
        gw = jnp.zeros((512, 256), F32)
        for r in range(ROWS):
            p = es_v[part, r] * scale[2 * r + 1]
            gap = p - ea_v[part, r] * scale[2 * r]
            gc = gc + dot(jnp.concatenate(split2(p), axis=0), cx_v[r], 1, 1)
            hi, low = split2(gap)
            gw = gw + dot(jnp.concatenate([hi, low], axis=0), ftile_v[r], 1, 1)
            gh_v[r, 256 * part : 256 * part + 256, :] = hi
            gl_v[r, 256 * part : 256 * part + 256, :] = low
        both = gc[0:256] + gc[256:512]
        rate_mass = jnp.sum(both[:, 128:256], axis=1, keepdims=True)
        gb = both[:, 0:128] - jnp.exp(b) * rate_mass
        wide = (gw[256:512, 128:256] + gw[256:512, 0:128]) + gw[0:256, 128:256]
        return (
            gb.reshape(2, 16, 8, 128),
            packed_rows(wide + gw[0:256, 0:128]).reshape(2, 16, 128),
        )

    def backward_all(ev, total):
        scale = scales(total)
        gb, gw = backward(ev, 1, scale[1])
        sb_v[ev, 2:4, :, 0:8, :] = gb
        sb_v[ev, 2:4, :, 8, :] = gw
        send(
            sb_v.at[ev, 2:4, :, pl.ds(0, SLOT), :], cb_v.at[ev, :, :, pl.ds(0, SLOT), :],
            cb_s.at[ev], cb_r.at[ev], partner,
        )
        gb, gw = backward(ev, 0, scale[0])
        settle(cb_v.at[ev, :, :, pl.ds(0, SLOT), :], cb_r.at[ev])
        sb_v[ev, 0:2, :, 0:8, :] = gb + cb_v[ev, :, :, 0:8, :]
        sb_v[ev, 0:2, :, 8, :] = gw + cb_v[ev, :, :, 8, :]
        for t in turns:
            to = chip_at(*t)
            send(
                sb_v.at[ev, 0:2, to, pl.ds(0, SLOT), :],
                xr_v.at[ev, :, chip, pl.ds(0, SLOT), :],
                x_s.at[ev], x_r.at[ev], (2 * to + core, z),
            )

    def field_lik(r):
        both = dot(w128_v[...], gh_v[r], 0, 0) + dot(w128_v[...], gl_v[r], 0, 0)
        return ((both[32:48] + both[16:32]) + both[0:16]) * LN2

    def fifteen(ev):
        return xr_v.at[ev, :, pl.ds(0, NQ - 1), pl.ds(0, SLOT), :]

    def seven(ev):
        return zb_v.at[ev, pl.ds(0, 7), :, pl.ds(0, SLOT + 1), :]

    def piece_start(ev, extra):
        settle(fifteen(ev), x_r.at[ev])
        for n in range(2):
            xr_v[ev, n, chip, 0:SLOT, :] = sb_v[ev, n, chip, 0:SLOT, :]
            acc = xr_v[ev, n, 0, 0:SLOT, :]
            for q in range(1, NQ):
                acc = acc + xr_v[ev, n, q, 0:SLOT, :]
            zb_v[ev, z, n, 0:SLOT, :] = acc
            zb_v[ev, z, n, SLOT : SLOT + 1, :] = jnp.full((1, 128), extra, F32)
        mine = zb_v.at[ev, z, :, pl.ds(0, SLOT + 1), :]
        for k in far_order:
            send(mine, mine, zb_s.at[ev], zb_r.at[ev], zpeer(k))

    def piece_total(ev, n):
        total = zb_v[ev, 0, n, 0 : SLOT + 1, :]
        for k in range(1, NZ):
            total = total + zb_v[ev, k, n, 0 : SLOT + 1, :]
        return total[0:SLOT], total[SLOT : SLOT + 1]

    field_pieces()
    for r in range(ROWS):
        count_copies[r].wait()
        counts = cint_v[r].astype(F32).astype(BF16)
        e_parts = split3(rowv_v[1, r : r + 1, :])
        cx_v[r, 0:128, :] = counts
        cx_v[r, 128:256, :] = expand(e_parts, (128, WIDE))
        for j in range(1, 4):
            ks_v[r, 128 * j : 128 * j + 128, :] = counts
    backward_all(0, forward_first())
    prior(0)
    for r in range(ROWS):
        mom = fm_v[:, r, :] + 0.025 * (prior_v[r] + field_lik(r))
        hfield_v[r] = mom
        new = fcur_v[r] + 0.05 * mom
        fcur_v[r] = new
        nf_v[:, r, :] = new
    hs_v[1, 0] = fcur_v[ROWS - 1]
    hs_v[1, 1] = fcur_v[0]
    send(hs_v.at[1, 0], hr_v.at[1, 0], halo_s.at[1, 0], halo_r.at[1, 0], nxt)
    send(hs_v.at[1, 1], hr_v.at[1, 1], halo_s.at[1, 1], halo_r.at[1, 1], prv)
    piece_start(0, jnp.float32(0.0))
    field_pieces()
    energy = prior(1)

    pull = jnp.where(iota((SLOT, 128), 0) < 8, 0.25, 1.0)
    for n in range(2):
        @pl.when(4 * n + chip // 4 != z)
        def _():
            settle(mp_v.at[n, pl.ds(0, SLOT), :], mp_r.at[n])

    settle(seven(0), zb_r.at[0])
    for n in range(2):
        lik, _ = piece_total(0, n)
        q0 = q_v[0, n, chip, 0:SLOT, :]
        half_q = mp_v[n, 0:SLOT, :] + 0.001 * (lik - pull * q0)
        half_v[n, 0:SLOT, :] = half_q
        q_v[1, n, chip, 0:SLOT, :] = q0 + 0.002 * half_q
    mine = q_v.at[1, 0:2, chip, pl.ds(0, SLOT), :]
    for t in turns:
        send(mine, mine, s3_s, s3_r, (2 * chip_at(*t) + core, z))
    settle(q_v.at[1, 0:2, pl.ds(0, NQ - 1), pl.ds(0, SLOT), :], s3_r)
    send(own_set(1), other_set(1), f3_s, f3_r, partner)
    total = forward_second()
    backward_all(1, total)
    log_dens = jnp.zeros((1, WIDE), F32)
    for r in range(ROWS):
        log_mix = total[2 * r][0] * LN2 + jnp.log(total[2 * r][1])
        log_joint = total[2 * r + 1][0] * LN2 + jnp.log(total[2 * r + 1][1])
        log_dens = log_dens + rowv_v[0, r : r + 1, :] * (log_joint - log_mix)
    log_part = jnp.sum(log_dens) - energy
    square = jnp.zeros((FAC, WIDE), F32)
    for r in range(ROWS):
        last = hfield_v[r] + 0.025 * (prior_v[r] + field_lik(r))
        nfm_v[:, r, :] = last
        square = square + last * last
    piece_start(1, 0.5 * jnp.sum(square) - log_part)

    settle(seven_shards(0), ag_s)
    settle(seven_shards(0), fw_s)

    @pl.when(mom_owner)
    def _():
        settle(pm_v.at[pl.ds(0, 7), pl.ds(0, SLOT), :], mp_s)

    for ev in range(2):
        settle(cb_v.at[ev, :, :, pl.ds(0, SLOT), :], cb_s.at[ev])
        settle(fifteen(ev), x_s.at[ev])
        settle(seven(ev), zb_s.at[ev])
        for n in range(2):
            settle(hs_v.at[ev, n], halo_s.at[ev, n])
    settle(q_v.at[1, 0:2, pl.ds(0, NQ - 1), pl.ds(0, SLOT), :], s3_s)
    settle(own_set(1), f3_s)
    settle(ls_v.at[0], land_s.at[0])
    settle(ls_v.at[1], land_s.at[1])
    ours, theirs = q_v[1, side, span, 0:8, :], q_v[1, 2 + side, span, 0:8, :]
    nb_v[0:32, :] = jnp.where(core == 0, ours, theirs).reshape(32, 128)
    nb_v[32:64, :] = jnp.where(core == 0, theirs, ours).reshape(32, 128)
    ours, theirs = q_v[1, side, span, 8, :], q_v[1, 2 + side, span, 8, :]
    low, high = jnp.where(core == 0, ours, theirs), jnp.where(core == 0, theirs, ours)
    nw_v[...] = unpack_loadings(jnp.concatenate([low, high], axis=0))
    settle(seven(1), zb_r.at[1])
    weighed = jnp.zeros((SLOT, 128), F32)
    scalar = jnp.zeros((1, 128), F32)
    for n in range(2):
        lik, scalar = piece_total(1, n)
        q1 = q_v[1, n, chip, 0:SLOT, :]
        mom = half_v[n, 0:SLOT, :] + 0.001 * (lik - pull * q1)
        half_v[n, 0:SLOT, :] = mom
        weighed = weighed + 0.5 * (mom * mom) + (0.5 * pull) * (q1 * q1)
    sc_v[c] = scalar + jnp.sum(weighed)

    @pl.when(mom_owner)
    def _():
        mo_v[mom_piece, 0:SLOT, :] = half_v[side, 0:SLOT, :]
        for peer in everyone:
            send(sc_v.at[c], sc_v.at[c], sc_s, sc_r, peer)
            send(
                half_v.at[side, pl.ds(0, SLOT), :], mo_v.at[mom_piece, pl.ds(0, SLOT), :],
                mo_s, mo_r, peer,
            )
        settle(mo_v.at[pl.ds(0, 7), pl.ds(0, SLOT), :], mo_r)

    @pl.when(jnp.logical_not(mom_owner))
    def _():
        for peer in everyone:
            send(sc_v.at[c], sc_v.at[c], sc_s, sc_r, peer)
        settle(mo_v.at[:, pl.ds(0, SLOT), :], mo_r)

    mo_o[:, 0:SLOT, :] = mo_v[:, 0:SLOT, :]
    settle(sc_v.at[pl.ds(0, NC - 1)], sc_r)
    sc_o[...] = sc_v[...]

    settle(sc_v.at[pl.ds(0, NC - 1)], sc_s)

    @pl.when(mom_owner)
    def _():
        settle(tally_v.at[:, pl.ds(0, SLOT), :], mo_s)


def hand_over(
    nf_v, nb_v, nw_v, nfm_v, mo_v, sc_v,
    nf_hbm, nb_hbm, nw_hbm, nfm_hbm, nbm_hbm, nwm_hbm, ham_hbm, nbm_v, nwm_v, ham_v, sem,
):
    moves = (
        (nf_v, nf_hbm), (nb_v, nb_hbm), (nw_v, nw_hbm), (nfm_v, nfm_hbm),
        (nbm_v, nbm_hbm), (nwm_v, nwm_hbm), (ham_v, ham_hbm),
    )
    copies = [pltpu.make_async_copy(s, d, sem.at[i]) for i, (s, d) in enumerate(moves)]
    for cp in copies[:4]:
        cp.start()
    nbm_v[...] = mo_v[:, 0:8, :].reshape(64, 128)
    nwm_v[...] = unpack_loadings(mo_v[:, 8, :])
    total = sc_v[0]
    for k in range(1, NC):
        total = total + sc_v[k]
    ham_v[...] = total * (1.0 / 262144.0)
    for cp in copies[4:]:
        cp.start()
    for cp in copies:
        cp.wait()


def per_device(
    factor_field, profile, mixing, factor_mom, profile_mom, mixing_mom, field_tau,
    counts, land_mask, log_exposure,
):
    hbm = pl.BlockSpec(memory_space=pltpu.MemorySpace.HBM)
    near = pl.BlockSpec(memory_space=pltpu.MemorySpace.VMEM)
    vm = pltpu.VMEM
    dma = pltpu.SemaphoreType.DMA
    shapes = [
        jax.ShapeDtypeStruct(a.shape, F32)
        for a in (factor_field, profile, mixing, factor_mom, profile_mom, mixing_mom)
    ]
    shapes.append(jax.ShapeDtypeStruct((1, 128), F32))
    scratch = [
        vm((FAC, ROWS, WIDE), F32), vm((64, 128), F32), vm((FAC, 64), F32),
        vm((FAC, ROWS, WIDE), F32), vm((64, 128), F32), vm((FAC, 64), F32),
        vm((ROWS, 128, WIDE), jnp.int32), vm((32, WIDE), jnp.int32), vm((32, WIDE), F32),
        vm((2, 4, NQ, 16, 128), F32), vm((8, 16, 128), F32), vm((2, 16, 128), F32),
        vm((2, 16, 128), F32), vm((8, 16, 128), F32), vm((ROWS, 256, WIDE), BF16),
        vm((ROWS, 512, WIDE), BF16), vm((2, 8, WIDE), F32), vm((ROWS, 256, WIDE), BF16),
        vm((384, 128), BF16), vm((512, 128), BF16),
        vm((ROWS, FAC, WIDE), F32), vm((ROWS, FAC, WIDE), F32), vm((ROWS, FAC, WIDE), F32),
        vm((2, ROWS, 256, WIDE), F32), vm((2, ROWS, 256, WIDE), F32),
        vm((ROWS, 512, WIDE), BF16), vm((ROWS, 512, WIDE), BF16),
        vm((2, 4, NQ, 16, 128), F32), vm((2, 2, NQ, 16, 128), F32),
        vm((2, 2, NQ, 16, 128), F32), vm((2, NZ, 2, 16, 128), F32),
        vm((2, 2, FAC, WIDE), F32), vm((2, 2, FAC, WIDE), F32),
        vm((2, 1, WIDE), F32), vm((2, 1, WIDE), F32), vm((NC, 1, 128), F32),
        vm((NC - 1, 16, 128), F32), pltpu.SMEM((FAC,), F32),
        dma((9,)), dma((ROWS,)), dma, dma((NZ,)), dma, dma, dma, dma((2,)),
        dma((2,)), dma((2,)), dma((2,)), dma((2,)), dma((2,)), dma((2,)),
        dma, dma, dma, dma, dma((2, 2)), dma((2, 2)), dma((2,)), dma((2,)),
        dma, dma, dma, dma,
    ]
    outs = pl.pallas_call(
        leap_kernel,
        out_shape=[vm(s.shape, F32) for s in shapes[:4]]
        + [vm((8, 16, 128), F32), vm((NC, 1, 128), F32)],
        in_specs=[hbm] * 10,
        out_specs=[near] * 6,
        scratch_shapes=scratch,
        compiler_params=pltpu.CompilerParams(
            collective_id=0, has_side_effects=True, vmem_limit_bytes=56 * 1024 * 1024
        ),
        name="leapfrog",
    )(
        field_tau, factor_field, profile, mixing, factor_mom, profile_mom, mixing_mom,
        counts, land_mask, log_exposure,
    )
    outs = pl.pallas_call(
        hand_over,
        out_shape=shapes,
        in_specs=[near] * 6,
        out_specs=[hbm] * 7,
        scratch_shapes=[vm((64, 128), F32), vm((FAC, 64), F32), vm((1, 128), F32), dma((7,))],
        name="hand_over",
    )(*[pltpu.with_memory_space_constraint(o, pltpu.MemorySpace.VMEM) for o in outs])
    return (*outs[:6], outs[6][0, 0])


def solution(mesh):
    rows = P(None, ("cells", "comp"), None)
    ins = (
        rows, P("comp", None), P(None, "comp"), rows, P("comp", None), P(None, "comp"),
        P(), P(None, "cells", None), P("cells", None), P("cells", None),
    )
    outs = (
        rows, P("comp", None), P(None, "comp"), rows, P("comp", None), P(None, "comp"), P(),
    )
    return jax.shard_map(per_device, mesh=mesh, in_specs=ins, out_specs=outs, check_vma=False)
```
